32 devices in a mesh: dp: 2 (over x), row: 4 (over z), col: 4 (over y, core).
Axes of the slice: x: 2, y: 2, z: 4, core: 2. Of those that a mesh axis runs over, the one named last changes fastest.
Arguments:
- block_input: bfloat16 [8192, 1024], P(('dp', 'col'), 'row'), may hold values from -40 to 40
- w_qkv: bfloat16 [1024, 3, 1024], P('row', None, 'col'), may hold values from -0.1875 to 0.1875
- b_qv: float32 [2, 1024], P(None, 'col'), may hold values from -3 to 3
- w_out: bfloat16 [1024, 1024], P('col', 'row'), may hold values from -1.5 to 1.5
- b_out: float32 [1024], P('row'), may hold values from -3 to 3
- gain_one: float32 [1024], P('row'), may hold values from 0.5 to 1.5
- shift_one: float32 [1024], P('row'), may hold values from -3 to 3
- gain_two: float32 [1024], P('row'), may hold values from 0.5 to 1.5
- shift_two: float32 [1024], P('row'), may hold values from -3 to 3
- w_up: bfloat16 [1024, 4096], P('row', 'col'), may hold values from -0.1875 to 0.1875
- b_up: float32 [4096], P('col'), may hold values from -3 to 3
- w_down: bfloat16 [4096, 1024], P('col', 'row'), may hold values from -0.09375 to 0.09375
- b_down: float32 [1024], P('row'), may hold values from -3 to 3
- cotangent: bfloat16 [8192, 1024], P(('dp', 'col'), 'row'), may hold values from -12 to 12
Outputs:
- block_output: bfloat16 [8192, 1024], P(('dp', 'col'), 'row')
- grad_input: float32 [8192, 1024], P(('dp', 'col'), 'row')
- grad_w_qkv: float32 [1024, 3, 1024], P('row', None, 'col')
- grad_b_qv: float32 [2, 1024], P(None, 'col')
- grad_w_out: float32 [1024, 1024], P('col', 'row')
- grad_b_out: float32 [1024], P('row')
- grad_gain_one: float32 [1024], P('row')
- grad_shift_one: float32 [1024], P('row')
- grad_gain_two: float32 [1024], P('row')
- grad_shift_two: float32 [1024], P('row')
- grad_w_up: float32 [1024, 4096], P('row', 'col')
- grad_b_up: float32 [4096], P('col')
- grad_w_down: float32 [4096, 1024], P('col', 'row')
- grad_b_down: float32 [1024], P('row')
The draws below stay inside these ranges and needn't reach their ends.
All inputs are finite; a program needn't handle non-finite values.
Results may differ from the reference program's by a relative error of at most 0.0088.
Values may be sent and summed in bfloat16 or wider, within the bound.
No kernel may reach another device: no remote copies, remote signals or barrier semaphores. Data moves between devices by JAX's collectives and lax.ppermute only.
A program may use at most 128 MiB of HBM per device.

```python
import jax
import jax.numpy as jnp
from jax import lax

D = 1024
HEADS = 16
HD = 64
FF = 4096
LEN = 512
TOKENS = 8192
N_DP = 2


def draw_block_input(key, part):
    feature = jnp.exp(jnp.log(3.0) * jnp.arange(D, dtype=jnp.float32) / D)
    base = jax.random.truncated_normal(key, -4.0, 4.0, (TOKENS, D), jnp.float32)
    return (base * feature * 0.6).astype(jnp.bfloat16)


def draw_cotangent(key, part):
    feature = jnp.exp(jnp.log(3.0) * jnp.arange(D, dtype=jnp.float32) / D)
    token = jnp.exp(jnp.log(3.0) * jnp.arange(TOKENS, dtype=jnp.float32) / TOKENS)[:, None]
    base = jax.random.truncated_normal(key, -4.0, 4.0, (TOKENS, D), jnp.float32)
    return (base * feature * token / 3.0).astype(jnp.bfloat16)


def steps_of(rng, shape, pieces, least, largest):
    factor_of, own = 1.0, jax.random.fold_in(rng, 6)
    for axis_at, blocks in pieces:
        heights = jnp.exp(jax.random.uniform(jax.random.fold_in(own, axis_at), (blocks,), jnp.float32, least / len(pieces), largest / len(pieces)))
        factor_of = factor_of * jnp.repeat(heights, shape[axis_at] // blocks).reshape([-1 if axis == axis_at else 1 for axis in range(len(shape))])
    return factor_of


def normal_values(key, extent, spread, reach, shards=(), held_as=jnp.bfloat16):
    entries = jax.random.normal(key, extent, jnp.float32) * spread
    if len(shards) > 0:
        entries = steps_of(key, extent, shards, -0.22, 0.18) * entries
    return jnp.clip(entries, min=-reach, max=reach).astype(held_as)


def setup_inputs(seed: int = 0) -> dict:
    seeds = jax.random.split(jax.random.key(seed), 15)
    block_input = draw_block_input(jax.random.fold_in(seeds[14], 71), 0)
    w_qkv = normal_values(seeds[1], (D, 3, D), D ** -0.5, 0.1875, ((0, 4), (2, 4)))
    b_qv = normal_values(seeds[2], (2, D), 0.5, 3.0, ((1, 4),), jnp.float32)
    w_out = normal_values(seeds[3], (D, D), (D // 64) ** -0.5, 1.5, ((0, 4), (1, 4)))
    b_out = normal_values(seeds[4], (D,), 0.5, 3.0, ((0, 4),), jnp.float32)
    gain_one = jnp.clip(1.0 + 0.1 * jax.random.normal(seeds[5], (D,), jnp.float32), 0.5, 1.5)
    shift_one = normal_values(seeds[6], (D,), 0.5, 3.0, ((0, 4),), jnp.float32)
    gain_two = jnp.clip(1.0 + 0.1 * jax.random.normal(seeds[7], (D,), jnp.float32), 0.5, 1.5)
    shift_two = normal_values(seeds[8], (D,), 0.5, 3.0, ((0, 4),), jnp.float32)
    w_up = normal_values(seeds[9], (D, FF), D ** -0.5, 0.1875, ((0, 4), (1, 4)))
    b_up = normal_values(seeds[10], (FF,), 0.5, 3.0, ((0, 4),), jnp.float32)
    w_down = normal_values(seeds[11], (FF, D), FF ** -0.5, 0.09375, ((0, 4), (1, 4)))
    b_down = normal_values(seeds[12], (D,), 0.5, 3.0, ((0, 4),), jnp.float32)
    cotangent = draw_cotangent(jax.random.fold_in(seeds[14], 71), 0)
    return {"block_input": block_input, "w_qkv": w_qkv, "b_qv": b_qv, "w_out": w_out, "b_out": b_out, "gain_one": gain_one, "shift_one": shift_one, "gain_two": gain_two, "shift_two": shift_two, "w_up": w_up, "b_up": b_up, "w_down": w_down, "b_down": b_down, "cotangent": cotangent}


EPS = 1e-05

@jax.custom_vjp
def low(v):
    return lax.optimization_barrier(v.astype(jnp.bfloat16)).astype(jnp.float32)

@jax.custom_vjp
def low_back(v):
    return v

def low_keep(v):
    return (low(v), None)

def low_pass(kept, grad):
    return (grad,)

def back_keep(v):
    return (v, None)

def back_low(kept, grad):
    return (low(grad),)
low.defvjp(low_keep, low_pass)
low_back.defvjp(back_keep, back_low)

def layer_norm(values, gain, shift):
    mean = lax.optimization_barrier(jnp.mean(values, axis=-1, keepdims=True))
    variance = lax.optimization_barrier(jnp.mean(jnp.square(values - mean), axis=-1, keepdims=True))
    return (values - mean) * lax.rsqrt(variance + EPS) * gain + shift

def product(left, right):
    return jnp.dot(left, right, precision=lax.Precision.HIGHEST)

def attend(item):
    query, key, value = item
    scores = jnp.einsum('qhd,khd->hqk', query, key, precision=lax.Precision.HIGHEST)
    scores = low_back(scores * 0.125)
    rows = lax.broadcasted_iota(jnp.int32, scores.shape, 1)
    cols = lax.broadcasted_iota(jnp.int32, scores.shape, 2)
    scores = jnp.where(cols <= rows, scores, -1e+30)
    probs = low(jax.nn.softmax(scores, axis=-1))
    return jnp.einsum('hqk,khd->qhd', probs, value, precision=lax.Precision.HIGHEST)

def forward(inputs, w_qkv, b_qv, w_out, b_out, gain_one, shift_one, gain_two, shift_two, w_up, b_up, w_down, b_down):
    seq_count = inputs.shape[0] // LEN
    normed_one = low(layer_norm(inputs, gain_one, shift_one))
    bias_full = jnp.stack([b_qv[0], jnp.zeros_like(b_qv[0]), b_qv[1]])
    mixed = product(normed_one, w_qkv.reshape(D, 3 * D)).reshape(-1, 3, D) + bias_full
    mixed = low(low_back(mixed)).reshape(seq_count, LEN, 3, HEADS, HD)
    attended = lax.map(jax.checkpoint(attend), (mixed[:, :, 0], mixed[:, :, 1], mixed[:, :, 2]))
    attended = low(low_back(attended.reshape(-1, D)))
    hidden = inputs + low_back(product(attended, w_out) + b_out)
    normed_two = low(layer_norm(hidden, gain_two, shift_two))
    pre_act = low_back(product(normed_two, w_up) + b_up)
    act = low(jax.nn.gelu(pre_act, approximate=True))
    return hidden + low_back(product(act, w_down) + b_down)

def reference(block_input, w_qkv, b_qv, w_out, b_out, gain_one, shift_one, gain_two, shift_two, w_up, b_up, w_down, b_down, cotangent):
    params = tuple((p.astype(jnp.float32) for p in (w_qkv, b_qv, w_out, b_out, gain_one, shift_one, gain_two, shift_two, w_up, b_up, w_down, b_down)))
    group_tokens = TOKENS // N_DP
    inputs = block_input.astype(jnp.float32).reshape(N_DP, group_tokens, D)
    grads = cotangent.astype(jnp.float32).reshape(N_DP, group_tokens, D)

    def step(carry, item):
        values, grad_out = item
        result, pull = jax.vjp(forward, values, *params)
        pulled = pull(grad_out)
        return (tuple((a + b for a, b in zip(carry, pulled[1:]))), (result.astype(jnp.bfloat16), pulled[0]))
    start = tuple((jnp.zeros(p.shape, jnp.float32) for p in params))
    totals, (results, grad_inputs) = lax.scan(step, start, (inputs, grads))
    return (results.reshape(TOKENS, D), grad_inputs.reshape(TOKENS, D), totals[0], totals[1], totals[2], totals[3], totals[4], totals[5], totals[6], totals[7], totals[8], totals[9], totals[10], totals[11])
```

```python
from functools import partial

import jax
import jax.numpy as jnp
from jax import lax
from jax.experimental import pallas as pl
from jax.experimental.pallas import tpu as pltpu
from jax.sharding import PartitionSpec as P

HD = 64
LEN = 512
EPS = 1e-05
MASKED = -1e30
F32 = jnp.float32
BF16 = jnp.bfloat16
N = 4


def dot(a, b, ca=1, cb=0):
    return lax.dot_general(a, b, (((ca,), (cb,)), ((), ())), preferred_element_type=F32)


def head_mask(shape, h):
    return lax.broadcasted_iota(jnp.int32, shape, 1) // HD == h


def attn_fwd_kernel(core_ref, proj_ref, out_ref, lse_ref):
    half, width = LEN // 2, out_ref.shape[1]
    core = core_ref[0]
    r0 = pl.ds(pl.multiple_of(core * half, half), half)
    r1 = pl.ds(pl.multiple_of((1 - core) * half, half), half)
    q0, q1 = proj_ref[r0, :width], proj_ref[r1, :width]
    k0, k1 = proj_ref[r0, width : 2 * width], proj_ref[r1, width : 2 * width]
    v0, v1 = proj_ref[r0, 2 * width :], proj_ref[r1, 2 * width :]
    tri = lax.broadcasted_iota(jnp.int32, (half, half), 1) <= lax.broadcasted_iota(
        jnp.int32, (half, half), 0
    )
    out0 = jnp.zeros((half, width), F32)
    out1 = jnp.zeros((half, width), F32)
    lse0 = jnp.zeros((half, 128), F32)
    lse1 = jnp.zeros((half, 128), F32)
    lane = lax.broadcasted_iota(jnp.int32, (half, 128), 1)
    for h in range(width // HD):
        mask = head_mask((half, width), h)
        zero = jnp.zeros((half, width), BF16)
        qh0, qh1 = jnp.where(mask, q0, zero), jnp.where(mask, q1, zero)
        vh0, vh1 = jnp.where(mask, v0, zero), jnp.where(mask, v1, zero)
        s00 = jnp.where(tri, dot(qh0, k0, 1, 1) * 0.125, MASKED)
        top = jnp.max(s00, axis=1, keepdims=True)
        e00 = jnp.exp(s00 - top)
        total = jnp.sum(e00, axis=1, keepdims=True)
        out0 += dot((e00 / total).astype(BF16), vh0)
        lse0 = jnp.where(lane == h, top + jnp.log(total), lse0)
        s10 = dot(qh1, k0, 1, 1) * 0.125
        s11 = jnp.where(tri, dot(qh1, k1, 1, 1) * 0.125, MASKED)
        top = jnp.maximum(
            jnp.max(s10, axis=1, keepdims=True), jnp.max(s11, axis=1, keepdims=True)
        )
        e10, e11 = jnp.exp(s10 - top), jnp.exp(s11 - top)
        total = jnp.sum(e10, axis=1, keepdims=True) + jnp.sum(e11, axis=1, keepdims=True)
        out1 += dot((e10 / total).astype(BF16), vh0) + dot((e11 / total).astype(BF16), vh1)
        lse1 = jnp.where(lane == h, top + jnp.log(total), lse1)
    out_ref[r0, :] = out0.astype(BF16)
    out_ref[r1, :] = out1.astype(BF16)
    lse_ref[r0, :] = lse0
    lse_ref[r1, :] = lse1


def attn_bwd_kernel(core_ref, proj_ref, lse_ref, grad_ref, out_ref):
    half, width = LEN // 2, grad_ref.shape[1]
    core = core_ref[0]
    r0 = pl.ds(pl.multiple_of(core * half, half), half)
    r1 = pl.ds(pl.multiple_of((1 - core) * half, half), half)
    q0, q1 = proj_ref[r0, :width], proj_ref[r1, :width]
    k0, k1 = proj_ref[r0, width : 2 * width], proj_ref[r1, width : 2 * width]
    v0, v1 = proj_ref[r0, 2 * width :], proj_ref[r1, 2 * width :]
    g0, g1 = grad_ref[r0, :], grad_ref[r1, :]
    lse0, lse1 = lse_ref[r0, :], lse_ref[r1, :]
    tri = lax.broadcasted_iota(jnp.int32, (half, half), 1) <= lax.broadcasted_iota(
        jnp.int32, (half, half), 0
    )
    zeros = jnp.zeros((half, width), F32)
    dq0, dq1, dk0, dk1, dv0, dv1 = (zeros,) * 6
    for h in range(width // HD):
        mask = head_mask((half, width), h)
        zero = jnp.zeros((half, width), BF16)
        qh0, qh1 = jnp.where(mask, q0, zero), jnp.where(mask, q1, zero)
        kh0, kh1 = jnp.where(mask, k0, zero), jnp.where(mask, k1, zero)
        gh0, gh1 = jnp.where(mask, g0, zero), jnp.where(mask, g1, zero)
        l0, l1 = lse0[:, h : h + 1], lse1[:, h : h + 1]
        p00 = jnp.exp(jnp.where(tri, dot(qh0, k0, 1, 1) * 0.125, MASKED) - l0)
        d00 = dot(gh0, v0, 1, 1)
        inner = jnp.sum(p00 * d00, axis=1, keepdims=True)
        t00 = (p00 * (d00 - inner)).astype(BF16)
        p10 = jnp.exp(dot(qh1, k0, 1, 1) * 0.125 - l1)
        p11 = jnp.exp(jnp.where(tri, dot(qh1, k1, 1, 1) * 0.125, MASKED) - l1)
        d10, d11 = dot(gh1, v0, 1, 1), dot(gh1, v1, 1, 1)
        inner = jnp.sum(p10 * d10, axis=1, keepdims=True) + jnp.sum(
            p11 * d11, axis=1, keepdims=True
        )
        t10 = (p10 * (d10 - inner)).astype(BF16)
        t11 = (p11 * (d11 - inner)).astype(BF16)
        p00, p10, p11 = p00.astype(BF16), p10.astype(BF16), p11.astype(BF16)
        dv0 += dot(p00, gh0, 0, 0) + dot(p10, gh1, 0, 0)
        dv1 += dot(p11, gh1, 0, 0)
        dq0 += dot(t00, kh0)
        dq1 += dot(t10, kh0) + dot(t11, kh1)
        dk0 += dot(t00, qh0, 0, 0) + dot(t10, qh1, 0, 0)
        dk1 += dot(t11, qh1, 0, 0)
    out_ref[r0, :width] = (dq0 * 0.125).astype(BF16)
    out_ref[r1, :width] = (dq1 * 0.125).astype(BF16)
    out_ref[r0, width : 2 * width] = (dk0 * 0.125).astype(BF16)
    out_ref[r1, width : 2 * width] = (dk1 * 0.125).astype(BF16)
    out_ref[r0, 2 * width :] = dv0.astype(BF16)
    out_ref[r1, 2 * width :] = dv1.astype(BF16)


SMEM = pl.BlockSpec(memory_space=pltpu.SMEM)
VMEM = pl.BlockSpec(memory_space=pltpu.VMEM)


def attn_fwd(core, proj):
    rows, width = proj.shape[0], proj.shape[1] // 3
    return pl.pallas_call(
        attn_fwd_kernel,
        out_shape=(
            jax.ShapeDtypeStruct((rows, width), BF16),
            jax.ShapeDtypeStruct((rows, 128), F32),
        ),
        in_specs=[SMEM, VMEM],
        out_specs=(VMEM, VMEM),
        name="attn_fwd",
    )(core, proj)


def attn_bwd(core, proj, lse, grad):
    return pl.pallas_call(
        attn_bwd_kernel,
        out_shape=jax.ShapeDtypeStruct(proj.shape, BF16),
        in_specs=[SMEM, VMEM, VMEM, VMEM],
        out_specs=VMEM,
        name="attn_bwd",
    )(core, proj, lse, grad)


def pp_y(v):
    return lax.ppermute(v, "col", [(i, i ^ 2) for i in range(N)])


def pp_c(v):
    return lax.ppermute(v, "col", [(i, i ^ 1) for i in range(N)])


def pp_x(v):
    return lax.ppermute(v, "dp", [(0, 1), (1, 0)])


def pp_z(v, s):
    return lax.ppermute(v, "row", [(i, (i + s) % N) for i in range(N)])


def pick(stacked, index):
    return lax.dynamic_index_in_dim(stacked, index, 0, keepdims=False)


def order_features(blocks):
    n_dp = lax.axis_size("dp")
    x = lax.axis_index("dp")
    size = blocks[0].shape[1] // n_dp
    parts = [[b[:, p * size : (p + 1) * size] for b in blocks] for p in range(n_dp)]
    if n_dp == 2:
        first = [jnp.where(x == 0, a, b) for a, b in zip(parts[0], parts[1])]
        second = [jnp.where(x == 0, b, a) for a, b in zip(parts[0], parts[1])]
        parts = [first, second]
    return jnp.concatenate([piece for part in parts for piece in part], axis=1)


def blocks_of(values):
    n_dp = lax.axis_size("dp")
    x = lax.axis_index("dp")
    width = values.shape[1] // N
    size = width // n_dp
    out = []
    for s in range(N):
        parts = [
            values[:, (p * N + s) * size : (p * N + s + 1) * size] for p in range(n_dp)
        ]
        if n_dp == 2:
            a, b = parts
            parts = [jnp.where(x == 0, a, b), jnp.where(x == 0, b, a)]
        out.append(jnp.concatenate(parts, axis=1))
    return out


def tokens_in(values):
    r, c = lax.axis_index("row"), lax.axis_index("col")
    rows = values.shape[0] // N
    pieces = []
    for t in range(N):
        sub = lax.dynamic_slice_in_dim(values, (r ^ t) * rows, rows, 0)
        pairs = [(i * N + j, j * N + (i ^ t)) for i in range(N) for j in range(N)]
        pieces.append(lax.ppermute(sub, ("row", "col"), pairs))
    stacked = jnp.stack(pieces)
    return order_features([pick(stacked, c ^ ((r - s) % N)) for s in range(N)])


def tokens_out(values):
    r, c = lax.axis_index("row"), lax.axis_index("col")
    stacked = jnp.stack(blocks_of(values))
    pieces = []
    for t in range(N):
        pairs = [(i * N + j, (j ^ t) * N + i) for i in range(N) for j in range(N)]
        pieces.append(lax.ppermute(pick(stacked, (r - (c ^ t)) % N), ("row", "col"), pairs))
    got = jnp.stack(pieces)
    return jnp.concatenate([pick(got, r ^ j) for j in range(N)], axis=0)


def gather_weight(shard, axis):
    n_dp = lax.axis_size("dp")
    x = lax.axis_index("dp")
    size = shard.shape[axis] // n_dp
    own = lax.dynamic_slice_in_dim(shard, x * size, size, axis)
    got = [own] + [pp_z(own, s) for s in range(1, N)]
    if n_dp == 2:
        other = lax.dynamic_slice_in_dim(shard, (1 - x) * size, size, axis)
        got += [other] + [pp_x(g) for g in got[1:]]
        return jnp.concatenate(got, axis=axis)
    whole = lax.all_gather(jnp.concatenate(got, axis=axis), "dp", axis=axis, tiled=True)
    return whole


def reduce_weight(grad_of, axis, width):
    n_dp = lax.axis_size("dp")
    x = lax.axis_index("dp")
    size = width // (n_dp * N)
    if n_dp == 2:
        sent = pp_x(grad_of(width // 2, width).astype(BF16))
        part = grad_of(0, width // 2) + sent.astype(F32)
    else:
        part = lax.psum_scatter(
            grad_of(0, width), "dp", scatter_dimension=axis, tiled=True
        )
    low = part.astype(BF16)
    total = lax.slice_in_dim(part, 0, size, axis=axis)
    for s in range(1, N):
        piece = lax.slice_in_dim(low, s * size, (s + 1) * size, axis=axis)
        total = total + pp_z(piece, N - s).astype(F32)
    total = total.astype(BF16)
    if n_dp == 2:
        other = pp_x(total)
        a, b = jnp.where(x == 0, total, other), jnp.where(x == 0, other, total)
        return jnp.concatenate([a, b], axis=axis).astype(F32)
    return lax.all_gather(total, "dp", axis=axis, tiled=True).astype(F32)


def gather_tokens(values):
    far = pp_y(values)
    near = jnp.concatenate([values, pp_c(values)], axis=0)
    return near, jnp.concatenate([far, pp_c(far)], axis=0)


def reduce_tokens(near, far):
    rows = near.shape[0] // 2
    far = far[:rows] + pp_c(far[rows:].astype(BF16)).astype(F32)
    far = pp_y(far.astype(BF16))
    near = near[:rows] + pp_c(near[rows:].astype(BF16)).astype(F32)
    return near + far.astype(F32)


def norm_forward(values, gain, shift):
    mean = jnp.mean(values, axis=1, keepdims=True)
    centred = values - mean
    scale = lax.rsqrt(jnp.mean(centred * centred, axis=1, keepdims=True) + EPS)
    normal = centred * scale
    return normal, scale, (normal * gain + shift).astype(BF16)


def norm_backward(grad, normal, scale, gain):
    scaled = grad * gain
    mean = jnp.mean(scaled, axis=1, keepdims=True)
    inner = jnp.mean(scaled * normal, axis=1, keepdims=True)
    return (scaled - mean - normal * inner) * scale, jnp.sum(grad * normal, 0), jnp.sum(grad, 0)


def body(
    block_input,
    w_qkv,
    b_qv,
    w_out,
    b_out,
    gain_one,
    shift_one,
    gain_two,
    shift_two,
    w_up,
    b_up,
    w_down,
    b_down,
    cotangent,
):
    r, c = lax.axis_index("row"), lax.axis_index("col")
    core = (c % 2).astype(jnp.int32).reshape(1)
    width_row = block_input.shape[1]
    width = width_row * N
    width_col = w_qkv.shape[2]
    hidden_col = w_up.shape[1]

    inputs = tokens_in(block_input).astype(F32)
    vectors = jnp.stack([gain_one, shift_one, gain_two, shift_two, b_out, b_down])
    vectors = order_features([vectors] + [pp_z(vectors, s) for s in range(1, N)])
    gain_one, shift_one, gain_two, shift_two, b_out, b_down = [vectors[i] for i in range(6)]
    qkv = gather_weight(w_qkv.reshape(width_row, 3 * width_col), 0)
    out_w = gather_weight(w_out, 1)
    up = gather_weight(w_up, 0)
    down = gather_weight(w_down, 1)
    grads = tokens_in(cotangent)
    grad_near, grad_far = gather_tokens(grads)

    normal_one, scale_one, normed_one = norm_forward(inputs, gain_one, shift_one)
    one_near, one_far = gather_tokens(normed_one)
    bias = jnp.concatenate([b_qv[0], jnp.zeros_like(b_qv[0]), b_qv[1]])

    def attend(normed):
        proj = (dot(normed, qkv) + bias).astype(BF16)
        att, lse = attn_fwd(core, proj)
        return proj, att, lse, dot(att, out_w)

    proj_near, att_near, lse_near, part_near = attend(one_near)
    proj_far, att_far, lse_far, part_far = attend(one_far)
    hidden = inputs + reduce_tokens(part_near, part_far) + b_out

    normal_two, scale_two, normed_two = norm_forward(hidden, gain_two, shift_two)
    two_near, two_far = gather_tokens(normed_two)

    def feed(normed, grad):
        pre = dot(normed, up) + b_up
        act, pull = jax.vjp(partial(jax.nn.gelu, approximate=True), pre)
        act = act.astype(BF16)
        grad_pre = pull(dot(grad, down, 1, 1))[0]
        sums = jnp.sum(grad_pre.astype(BF16).astype(F32), axis=0)
        grad_pre = grad_pre.astype(BF16)
        return act, grad_pre, dot(act, down), dot(grad_pre, up, 1, 1), sums

    act_near, pre_near, mlp_near, back_near, sum_near = feed(two_near, grad_near)
    act_far, pre_far, mlp_far, back_far, sum_far = feed(two_far, grad_far)
    grad_b_up = sum_near + sum_far
    grad_two = reduce_tokens(back_near, back_far)
    block_output = (hidden + reduce_tokens(mlp_near, mlp_far) + b_down).astype(BF16)
    block_output = tokens_out(block_output)

    def down_grad(lo, hi):
        return dot(act_near, grad_near[:, lo:hi], 0, 0) + dot(act_far, grad_far[:, lo:hi], 0, 0)

    def up_grad(lo, hi):
        return dot(two_near[:, lo:hi], pre_near, 0, 0) + dot(two_far[:, lo:hi], pre_far, 0, 0)

    grad_w_down = reduce_weight(down_grad, 1, width)
    grad_w_up = reduce_weight(up_grad, 0, width)

    norm_grad, grad_gain_two, grad_shift_two = norm_backward(
        grad_two, normal_two, scale_two, gain_two
    )
    grad_hidden = grads.astype(F32) + norm_grad
    branch = grad_hidden.astype(BF16)
    branch_near, branch_far = gather_tokens(branch)
    grad_b_out = jnp.sum(branch.astype(F32), axis=0)
    grad_b_down = jnp.sum(grads.astype(F32), axis=0)

    def attend_back(grad, proj, lse):
        grad_proj = attn_bwd(core, proj, lse, dot(grad, out_w, 1, 1).astype(BF16))
        return grad_proj, dot(grad_proj, qkv, 1, 1), jnp.sum(grad_proj.astype(F32), axis=0)

    gp_near, back_near, sum_near = attend_back(branch_near, proj_near, lse_near)
    gp_far, back_far, sum_far = attend_back(branch_far, proj_far, lse_far)
    sums = (sum_near + sum_far).reshape(3, width_col)

    def out_grad(lo, hi):
        return dot(att_near, branch_near[:, lo:hi], 0, 0) + dot(
            att_far, branch_far[:, lo:hi], 0, 0
        )

    def qkv_grad(lo, hi):
        return dot(one_near[:, lo:hi], gp_near, 0, 0) + dot(one_far[:, lo:hi], gp_far, 0, 0)

    grad_w_out = reduce_weight(out_grad, 1, width)
    grad_w_qkv = reduce_weight(qkv_grad, 0, width).reshape(width_row, 3, width_col)

    grad_one = reduce_tokens(back_near, back_far)
    norm_grad, grad_gain_one, grad_shift_one = norm_backward(
        grad_one, normal_one, scale_one, gain_one
    )
    grad_input = tokens_out((grad_hidden + norm_grad).astype(BF16)).astype(F32)

    by_feature = jnp.stack(
        [grad_gain_one, grad_shift_one, grad_gain_two, grad_shift_two, grad_b_out, grad_b_down]
    )
    by_feature = jnp.stack(blocks_of(by_feature))
    by_feature = jnp.concatenate([pick(by_feature, (r - i) % N) for i in range(N)], axis=1)
    by_col = jnp.concatenate([grad_b_up, sums[0], sums[2]])
    slots = jnp.where(jnp.arange(N)[:, None] == c, by_col[None, :], 0.0)
    by_feature, slots = lax.psum((by_feature, slots), ("dp", "row", "col"))
    by_feature = lax.dynamic_slice_in_dim(by_feature, r * width_row, width_row, 1)
    by_col = pick(slots, c)
    grad_b_up = by_col[:hidden_col]
    grad_b_qv = by_col[hidden_col:].reshape(2, width_col)
    return (
        block_output,
        grad_input,
        grad_w_qkv,
        grad_b_qv,
        grad_w_out,
        by_feature[4],
        by_feature[0],
        by_feature[1],
        by_feature[2],
        by_feature[3],
        grad_w_up,
        grad_b_up,
        grad_w_down,
        by_feature[5],
    )


def solution(mesh):
    assert mesh.shape["row"] == N and mesh.shape["col"] == N
    tokens = P(("dp", "col"), "row")
    placed = (
        tokens,
        P("row", None, "col"),
        P(None, "col"),
        P("col", "row"),
        P("row"),
        P("row"),
        P("row"),
        P("row"),
        P("row"),
        P("row", "col"),
        P("col"),
        P("col", "row"),
        P("row"),
        tokens,
    )
    return jax.shard_map(
        body,
        mesh=mesh,
        in_specs=placed,
        out_specs=(tokens, tokens) + placed[1:13],
        check_vma=False,
    )
```

```python
import jax
import jax.numpy as jnp
from jax import lax
from jax.experimental import pallas as pl
from jax.experimental.pallas import tpu as pltpu
from jax.sharding import PartitionSpec as P


HD = 64
LEN = 512
EPS = 1e-05
MASKED = -1e30
F32 = jnp.float32
BF16 = jnp.bfloat16
N = 4
EXTRA = 16


def dot(a, b, ca=1, cb=0):
    return lax.dot_general(a, b, (((ca,), (cb,)), ((), ())), preferred_element_type=F32)


def head_mask(shape, h):
    return lax.broadcasted_iota(jnp.int32, shape, 1) // HD == h


def attn_fwd(core, proj_ref, out_ref, lse_ref):
    half, width = LEN // 2, out_ref.shape[1]
    r0 = pl.ds(pl.multiple_of(core * half, half), half)
    r1 = pl.ds(pl.multiple_of((1 - core) * half, half), half)
    q0, q1 = proj_ref[r0, :width], proj_ref[r1, :width]
    k0, k1 = proj_ref[r0, width : 2 * width], proj_ref[r1, width : 2 * width]
    v0, v1 = proj_ref[r0, 2 * width :], proj_ref[r1, 2 * width :]
    tri = lax.broadcasted_iota(jnp.int32, (half, half), 1) <= lax.broadcasted_iota(
        jnp.int32, (half, half), 0
    )
    out0 = jnp.zeros((half, width), F32)
    out1 = jnp.zeros((half, width), F32)
    lse0 = jnp.zeros((half, 128), F32)
    lse1 = jnp.zeros((half, 128), F32)
    lane = lax.broadcasted_iota(jnp.int32, (half, 128), 1)
    for h in range(width // HD):
        mask = head_mask((half, width), h)
        zero = jnp.zeros((half, width), BF16)
        qh0, qh1 = jnp.where(mask, q0, zero), jnp.where(mask, q1, zero)
        vh0, vh1 = jnp.where(mask, v0, zero), jnp.where(mask, v1, zero)
        s00 = jnp.where(tri, dot(qh0, k0, 1, 1) * 0.125, MASKED)
        top = jnp.max(s00, axis=1, keepdims=True)
        e00 = jnp.exp(s00 - top)
        total = jnp.sum(e00, axis=1, keepdims=True)
        out0 += dot((e00 / total).astype(BF16), vh0)
        lse0 = jnp.where(lane == h, top + jnp.log(total), lse0)
        s10 = dot(qh1, k0, 1, 1) * 0.125
        s11 = jnp.where(tri, dot(qh1, k1, 1, 1) * 0.125, MASKED)
        top = jnp.maximum(
            jnp.max(s10, axis=1, keepdims=True), jnp.max(s11, axis=1, keepdims=True)
        )
        e10, e11 = jnp.exp(s10 - top), jnp.exp(s11 - top)
        total = jnp.sum(e10, axis=1, keepdims=True) + jnp.sum(e11, axis=1, keepdims=True)
        out1 += dot((e10 / total).astype(BF16), vh0) + dot((e11 / total).astype(BF16), vh1)
        lse1 = jnp.where(lane == h, top + jnp.log(total), lse1)
    out_ref[r0, :] = out0.astype(BF16)
    out_ref[r1, :] = out1.astype(BF16)
    lse_ref[r0, :] = lse0
    lse_ref[r1, :] = lse1


def attn_bwd(core, proj_ref, lse_ref, grad_ref, out_ref):
    half, width = LEN // 2, grad_ref.shape[1]
    r0 = pl.ds(pl.multiple_of(core * half, half), half)
    r1 = pl.ds(pl.multiple_of((1 - core) * half, half), half)
    q0, q1 = proj_ref[r0, :width], proj_ref[r1, :width]
    k0, k1 = proj_ref[r0, width : 2 * width], proj_ref[r1, width : 2 * width]
    v0, v1 = proj_ref[r0, 2 * width :], proj_ref[r1, 2 * width :]
    g0, g1 = grad_ref[r0, :], grad_ref[r1, :]
    lse0, lse1 = lse_ref[r0, :], lse_ref[r1, :]
    tri = lax.broadcasted_iota(jnp.int32, (half, half), 1) <= lax.broadcasted_iota(
        jnp.int32, (half, half), 0
    )
    zeros = jnp.zeros((half, width), F32)
    dq0, dq1, dk0, dk1, dv0, dv1 = (zeros,) * 6
    for h in range(width // HD):
        mask = head_mask((half, width), h)
        zero = jnp.zeros((half, width), BF16)
        qh0, qh1 = jnp.where(mask, q0, zero), jnp.where(mask, q1, zero)
        kh0, kh1 = jnp.where(mask, k0, zero), jnp.where(mask, k1, zero)
        gh0, gh1 = jnp.where(mask, g0, zero), jnp.where(mask, g1, zero)
        l0, l1 = lse0[:, h : h + 1], lse1[:, h : h + 1]
        p00 = jnp.exp(jnp.where(tri, dot(qh0, k0, 1, 1) * 0.125, MASKED) - l0)
        d00 = dot(gh0, v0, 1, 1)
        inner = jnp.sum(p00 * d00, axis=1, keepdims=True)
        t00 = (p00 * (d00 - inner)).astype(BF16)
        p10 = jnp.exp(dot(qh1, k0, 1, 1) * 0.125 - l1)
        p11 = jnp.exp(jnp.where(tri, dot(qh1, k1, 1, 1) * 0.125, MASKED) - l1)
        d10, d11 = dot(gh1, v0, 1, 1), dot(gh1, v1, 1, 1)
        inner = jnp.sum(p10 * d10, axis=1, keepdims=True) + jnp.sum(
            p11 * d11, axis=1, keepdims=True
        )
        t10 = (p10 * (d10 - inner)).astype(BF16)
        t11 = (p11 * (d11 - inner)).astype(BF16)
        p00, p10, p11 = p00.astype(BF16), p10.astype(BF16), p11.astype(BF16)
        dv0 += dot(p00, gh0, 0, 0) + dot(p10, gh1, 0, 0)
        dv1 += dot(p11, gh1, 0, 0)
        dq0 += dot(t00, kh0)
        dq1 += dot(t10, kh0) + dot(t11, kh1)
        dk0 += dot(t00, qh0, 0, 0) + dot(t10, qh1, 0, 0)
        dk1 += dot(t11, qh1, 0, 0)
    out_ref[r0, :width] = (dq0 * 0.125).astype(BF16)
    out_ref[r1, :width] = (dq1 * 0.125).astype(BF16)
    out_ref[r0, width : 2 * width] = (dk0 * 0.125).astype(BF16)
    out_ref[r1, width : 2 * width] = (dk1 * 0.125).astype(BF16)
    out_ref[r0, 2 * width :] = dv0.astype(BF16)
    out_ref[r1, 2 * width :] = dv1.astype(BF16)


SMEM = pl.BlockSpec(memory_space=pltpu.SMEM)
VMEM = pl.BlockSpec(memory_space=pltpu.VMEM)
ANY = pl.BlockSpec(memory_space=pl.ANY)


def shaped(shape, dtype):
    return jax.ShapeDtypeStruct(shape, dtype)


def vmem(mib=24):
    return pltpu.CompilerParams(vmem_limit_bytes=mib << 20)


def cost(flops):
    return pl.CostEstimate(flops=flops, transcendentals=0, bytes_accessed=4 << 20)


def piece_copies(place, refs, whole_ref, sems):
    x, r = place[0], place[1]
    own, *got = refs
    size = own.shape[0] // 2
    out = []

    def copy(source, part, row):
        at = pl.multiple_of((part * N + row) * size, size)
        out.append(pltpu.make_async_copy(source, whole_ref.at[pl.ds(at, size), :], sems.at[len(out)]))

    for p in range(2):
        copy(own.at[pl.ds(p * size, size), :], p, r)
    for s in range(1, N):
        copy(got[s - 1], x, (r + N - s) % N)
        copy(got[N - 2 + s], 1 - x, (r + N - s) % N)
    return out


def assemble(place, pieces):
    if len(pieces) == 1:
        return pieces[0]
    own = pieces[0]

    def assemble_kernel(place, *refs):
        *pieces, whole_ref, sems = refs
        copies = piece_copies(place, pieces, whole_ref, sems)
        for copy in copies:
            copy.start()
        for copy in copies:
            copy.wait()

    return pl.pallas_call(
        assemble_kernel,
        out_shape=shaped((N * own.shape[0], own.shape[1]), BF16),
        in_specs=[SMEM] + [ANY] * len(pieces),
        out_specs=VMEM,
        scratch_shapes=[pltpu.SemaphoreType.DMA((8,))],
        compiler_params=vmem(),
        cost_estimate=cost(1 << 20),
        name="assemble",
    )(place, *pieces)


def attend_kernel(
    place, a_ref, b_ref, w_ref, bias_ref, proj_ref, att_ref, lse_ref, p0_ref, p1_ref
):
    rows, wide = a_ref.shape[0], proj_ref.shape[1]
    weight = w_ref[:, :wide]
    both = jnp.concatenate([a_ref[...], b_ref[...]], axis=0)
    proj_ref[...] = (dot(both, weight) + bias_ref[...]).astype(BF16)
    attn_fwd(place[2], proj_ref, att_ref, lse_ref)
    weight = w_ref[:, wide:]
    part = dot(att_ref[...], weight, 1, 1)
    p0_ref[...] = part[:rows]
    p1_ref[...] = part[rows:].astype(BF16)


def attend(place, a, b, weight, bias):
    rows, width = a.shape
    wide = bias.shape[1]
    head = wide // 3
    return pl.pallas_call(
        attend_kernel,
        out_shape=(
            shaped((2 * rows, wide), BF16),
            shaped((2 * rows, head), BF16),
            shaped((2 * rows, 128), F32),
            shaped((rows, width), F32),
            shaped((rows, width), BF16),
        ),
        in_specs=[SMEM] + [VMEM] * 4,
        out_specs=(VMEM,) * 5,
        compiler_params=vmem(),
        cost_estimate=cost(16 * rows * width * width),
        name="attend",
    )(place, a, b, weight, bias)


def attend_back_kernel(place, *refs):
    a_ref, b_ref, na_ref, nb_ref, w_ref, proj_ref, lse_ref, *refs = refs
    gp_ref, p0_ref, p1_ref, sum_ref, feat_ref, grad_ref = refs
    rows, wide = a_ref.shape[0], proj_ref.shape[1]
    weight = w_ref[:, wide:]
    both = jnp.concatenate([a_ref[...], b_ref[...]], axis=0)
    grad_ref[...] = dot(both, weight).astype(BF16)
    attn_bwd(place[2], proj_ref, lse_ref, grad_ref, gp_ref)
    weight = w_ref[:, :wide]
    part = dot(gp_ref[...], weight, 1, 1)
    p0_ref[...] = part[:rows]
    p1_ref[...] = part[rows:].astype(BF16)
    sum_ref[...] = jnp.sum(gp_ref[...].astype(F32), axis=0, keepdims=True)
    feature_sums(feat_ref, part, na_ref, nb_ref, a_ref)


def feature_sums(feat_ref, part, na_ref, nb_ref, own_ref):
    normed = jnp.concatenate([na_ref[...], nb_ref[...]], axis=0).astype(F32)
    feat_ref[0:1, :] = jnp.sum(part * normed, axis=0, keepdims=True)
    feat_ref[1:2, :] = jnp.sum(part, axis=0, keepdims=True)
    feat_ref[2:3, :] = jnp.sum(own_ref[...].astype(F32), axis=0, keepdims=True)
    feat_ref[3:, :] = jnp.zeros((feat_ref.shape[0] - 3, feat_ref.shape[1]), F32)


def attend_back(place, a, b, na, nb, weight, proj, lse):
    rows, width = a.shape
    wide = proj.shape[1]
    return pl.pallas_call(
        attend_back_kernel,
        out_shape=(
            shaped((2 * rows, wide), BF16),
            shaped((rows, width), F32),
            shaped((rows, width), BF16),
            shaped((1, wide), F32),
            shaped((8, width), F32),
        ),
        in_specs=[SMEM] + [VMEM] * 7,
        out_specs=(VMEM,) * 5,
        scratch_shapes=[pltpu.VMEM((2 * rows, wide // 3), BF16)],
        compiler_params=vmem(),
        cost_estimate=cost(24 * rows * width * width),
        name="attend_back",
    )(place, a, b, na, nb, weight, proj, lse)


def feed_kernel(place, *refs):
    a_ref, b_ref, ga_ref, gb_ref, w_ref, bias_ref, *refs = refs
    act_ref, pre_ref, m0_ref, m1_ref, p0_ref, p1_ref, sum_ref, feat_ref = refs
    rows, hidden = a_ref.shape[0], act_ref.shape[1]
    size = 256
    normed = jnp.concatenate([a_ref[...], b_ref[...]], axis=0)
    grads = jnp.concatenate([ga_ref[...], gb_ref[...]], axis=0)
    for at in range(0, hidden, size):
        cols = slice(at, at + size)
        v = dot(normed, w_ref[:, cols]) + bias_ref[:, cols]
        root = 0.7978845608028654
        square = v * v
        t = jnp.tanh(root * (v + 0.044715 * (square * v)))
        half = 0.5 * (1.0 + t)
        act_ref[:, cols] = (v * half).astype(BF16)
        slope = half + 0.5 * v * (1.0 - t * t) * (root * (1.0 + 0.134145 * square))
        pre = (dot(grads, w_ref[:, hidden + at : hidden + at + size]) * slope).astype(BF16)
        pre_ref[:, cols] = pre
        sum_ref[:, cols] = jnp.sum(pre.astype(F32), axis=0, keepdims=True)
    part = dot(act_ref[...], w_ref[:, hidden:], 1, 1)
    m0_ref[...] = part[:rows]
    m1_ref[...] = part[rows:].astype(BF16)
    part = dot(pre_ref[...], w_ref[:, :hidden], 1, 1)
    p0_ref[...] = part[:rows]
    p1_ref[...] = part[rows:].astype(BF16)
    feature_sums(feat_ref, part, a_ref, b_ref, ga_ref)


def feed(place, a, b, grad_a, grad_b, weight, bias):
    rows, width = a.shape
    hidden = bias.shape[1]
    return pl.pallas_call(
        feed_kernel,
        out_shape=(
            shaped((2 * rows, hidden), BF16),
            shaped((2 * rows, hidden), BF16),
            shaped((rows, width), F32),
            shaped((rows, width), BF16),
            shaped((rows, width), F32),
            shaped((rows, width), BF16),
            shaped((1, hidden), F32),
            shaped((8, width), F32),
        ),
        in_specs=[SMEM] + [VMEM] * 6,
        out_specs=(VMEM,) * 8,
        compiler_params=vmem(),
        cost_estimate=cost(16 * rows * width * hidden),
        name="feed",
    )(place, a, b, grad_a, grad_b, weight, bias)


def weight_kernel(n_terms, place, *refs):
    terms, (*extra, sent_ref, kept_ref) = refs[: 6 * n_terms], refs[6 * n_terms :]
    step = pl.program_id(0)
    half = terms[0].shape[1]
    size = half // N
    stride = sent_ref.shape[0] // N

    def write(out_ref):
        start = 0
        for i in range(0, len(terms), 6):
            a, b, c, d, near, far = terms[i : i + 6]
            near_left = jnp.concatenate([a[...], b[...]], axis=0)
            far_left = jnp.concatenate([c[...], d[...]], axis=0)
            value = dot(near_left, near[...], 0, 0) + dot(far_left, far[...], 0, 0)
            value = value.astype(out_ref.dtype)
            cols = slice(start, start + near.shape[1])
            start = cols.stop
            for s in range(N):
                rows = slice(s * stride, s * stride + size)
                out_ref[rows, cols] = value[s * size : (s + 1) * size]
        if extra:
            write_extra(out_ref)

    def write_extra(out_ref):
        feat_ref, up_ref, qv_ref = extra
        cols = out_ref.shape[1]
        first = (place[0] + 1 + step) % 2 == 0
        for s in range(N):
            base = s * stride + size
            out_ref[base : base + EXTRA, :] = jnp.zeros((EXTRA, cols), out_ref.dtype)
            own = slice(s * size, (s + 1) * size)
            other = slice(half + s * size, half + (s + 1) * size)
            lanes = [
                jnp.where(first, feat_ref[v : v + 1, own], feat_ref[v : v + 1, other])
                for v in range(8)
            ]
            row = jnp.concatenate([up_ref[...], qv_ref[...]] + lanes, axis=1)
            for i in range(row.shape[1] // cols):
                piece = row[:, i * cols : (i + 1) * cols]
                high = piece.astype(BF16).astype(F32)
                at = base + 2 * i
                out_ref[at : at + 1, :] = high.astype(out_ref.dtype)
                out_ref[at + 1 : at + 2, :] = (piece - high).astype(out_ref.dtype)

    @pl.when(step == 0)
    def _():
        write(sent_ref)

    @pl.when(step == 1)
    def _():
        write(kept_ref)


def weight_grad(place, *terms, extra=()):
    args, specs, cols = [], [], 0
    rows, width = terms[0][0][0].shape
    half = width // 2
    for pieces, near, far, size, at in terms:
        args += [*pieces, near, far]
        specs += [pl.BlockSpec((rows, half), lambda i, ref: (0, (ref[0] + 1 + i) % 2))] * 4
        specs += [pl.BlockSpec((2 * rows, size), lambda i, ref, at=at: (0, at))] * 2
        cols += size
    specs += [pl.BlockSpec(e.shape, lambda i, ref: (0, 0)) for e in extra]
    tall = half + N * EXTRA if extra else half
    whole = pl.BlockSpec((tall, cols), lambda i, ref: (0, 0))
    return pl.pallas_call(
        lambda *refs: weight_kernel(len(terms), *refs),
        grid_spec=pltpu.PrefetchScalarGridSpec(
            num_scalar_prefetch=1, grid=(2,), in_specs=specs, out_specs=(whole, whole)
        ),
        out_shape=(shaped((tall, cols), BF16), shaped((tall, cols), F32)),
        compiler_params=vmem(),
        cost_estimate=cost(8 * rows * width * cols),
        name="weight_grad",
    )(place, *args, *extra)


def rows_kernel(place, a, b, c, d, near, far, *refs):
    *outs, value_ref = refs
    near_left = jnp.concatenate([a[...], b[...]], axis=0)
    far_left = jnp.concatenate([c[...], d[...]], axis=0)
    value_ref[...] = dot(near_left, near[...], 0, 0) + dot(far_left, far[...], 0, 0)
    size = value_ref.shape[0] // N
    to = pl.ds(pl.multiple_of(pl.program_id(0) * size, size), size)
    for shift, out_ref in enumerate(outs):
        at = pl.ds(pl.multiple_of(((place[1] + shift) % N) * size, size), size)
        out_ref[to, :] = value_ref[at, :].astype(out_ref.dtype)


def weight_rows(place, pieces, near, far):
    rows, width = pieces[0].shape
    half, cols = width // 2, near.shape[1]
    specs = [pl.BlockSpec((rows, half), lambda i, ref: (0, i))] * 4
    specs += [pl.BlockSpec((2 * rows, cols), lambda i, ref: (0, 0))] * 2
    whole = pl.BlockSpec((width // N, cols), lambda i, ref: (0, 0))
    out = shaped((width // N, cols), BF16)
    return pl.pallas_call(
        rows_kernel,
        grid_spec=pltpu.PrefetchScalarGridSpec(
            num_scalar_prefetch=1,
            grid=(2,),
            in_specs=specs,
            out_specs=(whole,) * N,
            scratch_shapes=[pltpu.VMEM((half, cols), F32)],
        ),
        out_shape=(shaped((width // N, cols), F32),) + (out,) * (N - 1),
        compiler_params=vmem(),
        cost_estimate=cost(8 * rows * width * cols),
        name="weight_rows",
    )(place, *pieces, near, far)


def combine_kernel(place, kept_ref, got_ref, own_ref, *outs):
    size, r = own_ref.shape[0], place[1]

    def block(shift):
        at = pl.ds(pl.multiple_of(((r + shift) % N) * size, size), size)
        return kept_ref[at, :] + got_ref[at, :].astype(F32)

    own_ref[...] = block(0)
    for shift, out_ref in enumerate(outs):
        out_ref[...] = block(shift + 1).astype(BF16)


def combine(place, kept, got):
    size, cols = kept.shape[0] // N, kept.shape[1]
    return pl.pallas_call(
        combine_kernel,
        out_shape=(shaped((size, cols), F32),) + (shaped((size, cols), BF16),) * (N - 1),
        in_specs=[SMEM, VMEM, VMEM],
        out_specs=(VMEM,) * N,
        compiler_params=vmem(),
        cost_estimate=cost(1 << 20),
        name="combine",
    )(place, kept, got)


def simple(kernel, outs, *args):
    return pl.pallas_call(
        kernel,
        out_shape=tuple(shaped(shape, dtype) for shape, dtype in outs),
        in_specs=[SMEM] + [VMEM] * (len(args) - 1),
        out_specs=(VMEM,) * len(outs),
        compiler_params=vmem(),
        cost_estimate=cost(1 << 20),
    )(*args)


def beside(place, first, second):
    rows, cols = first.shape[0], first.shape[1] + second.shape[0]

    def beside_kernel(place, a_ref, b_ref, out_ref):
        out_ref[:, : a_ref.shape[1]] = a_ref[...]
        out_ref[:, a_ref.shape[1] :] = b_ref[...].T

    return simple(beside_kernel, (((rows, cols), BF16),), place, first, second)[0]


def choose(index, refs, rows=slice(None)):
    value = refs[0][rows, :]
    for i in range(1, len(refs)):
        value = jnp.where(index == i, refs[i][rows, :], value)
    return value


def put_features(n_parts, out_ref, block, s, rows=slice(None)):
    size = block.shape[1] // n_parts
    for p in range(n_parts):
        at = (p * N + s) * size
        out_ref[rows, at : at + size] = block[:, p * size : (p + 1) * size]


def take_features(n_parts, values, s):
    size = values.shape[1] // N // n_parts
    parts = [values[:, (p * N + s) * size : (p * N + s + 1) * size] for p in range(n_parts)]
    return jnp.concatenate(parts, axis=1)


def moments(values):
    centred = values - jnp.mean(values, axis=1, keepdims=True)
    scale = lax.rsqrt(jnp.mean(centred * centred, axis=1, keepdims=True) + EPS)
    return centred * scale, scale


def enter(n_parts, place, pieces, n_vec):
    rows, width = (pieces[0].shape[0] - 32) // 2, pieces[0].shape[1] * N

    def enter_kernel(place, *refs):
        *pieces, x_ref, g_ref, vec_ref, normed_ref = refs
        vec_ref[...] = jnp.zeros_like(vec_ref)
        for s in range(N):
            block = choose(place[1] ^ s, pieces)
            put_features(n_parts, x_ref, block[:rows], s)
            put_features(n_parts, g_ref, block[rows : 2 * rows], s)
            terms = block[2 * rows :].astype(F32)
            vec = terms[:n_vec] + terms[n_vec : 2 * n_vec] + terms[2 * n_vec : 3 * n_vec]
            put_features(n_parts, vec_ref, vec, s, slice(0, n_vec))
        normal, _ = moments(x_ref[...].astype(F32))
        normed_ref[...] = (normal * vec_ref[0:1, :] + vec_ref[1:2, :]).astype(BF16)

    tokens = (rows, width), BF16
    outs = tokens, tokens, ((8, width), F32), tokens
    return simple(enter_kernel, outs, place, *pieces)


def split_tokens(place, first, second):
    rows, cols = first.shape[0] // N, first.shape[1]

    def split_kernel(place, a_ref, b_ref, *outs):
        for s, out_ref in enumerate(outs):
            at = pl.ds(pl.multiple_of((place[3] ^ s) * rows, rows), rows)
            out_ref[:rows, :] = a_ref[at, :]
            out_ref[rows:, :] = b_ref[at, :]

    return simple(split_kernel, (((2 * rows, cols), BF16),) * N, place, first, second)


def turn_tokens(place, pieces, extra=None):
    rows, cols = pieces[0].shape
    more = () if extra is None else (extra,)

    def turn_kernel(place, *refs):
        for t, out_ref in enumerate(refs[N + len(more) :]):
            out_ref[:rows, :] = choose(place[3] ^ place[1] ^ t, refs[:N])
            if more:
                out_ref[rows:, :] = refs[N][...]

    outs = (((rows + sum(e.shape[0] for e in more), cols), BF16),) * N
    return simple(turn_kernel, outs, place, *pieces, *more)


def summed(first_ref, second_ref, third_ref):
    return first_ref[...] + second_ref[...].astype(F32) + third_ref[...].astype(F32)


def middle(place, x, parts, vec):
    def middle_kernel(place, x_ref, a_ref, b_ref, c_ref, vec_ref, hidden_ref, normed_ref):
        hidden = x_ref[...].astype(F32) + summed(a_ref, b_ref, c_ref) + vec_ref[4:5, :]
        hidden_ref[...] = hidden
        normal, _ = moments(hidden)
        normed_ref[...] = (normal * vec_ref[2:3, :] + vec_ref[3:4, :]).astype(BF16)

    return simple(middle_kernel, ((x.shape, F32), (x.shape, BF16)), place, x, *parts, vec)


def norm_backward(grad, values, gain):
    normal, scale = moments(values)
    scaled = grad * gain
    mean = jnp.mean(scaled, axis=1, keepdims=True)
    inner = jnp.mean(scaled * normal, axis=1, keepdims=True)
    return (scaled - mean - normal * inner) * scale


def middle_back(place, hidden, grads, parts, vec):
    def middle_back_kernel(place, h_ref, g_ref, a_ref, b_ref, c_ref, vec_ref, out_ref, low_ref):
        grad = norm_backward(summed(a_ref, b_ref, c_ref), h_ref[...], vec_ref[2:3, :])
        grad = g_ref[...].astype(F32) + grad
        out_ref[...] = grad
        low_ref[...] = grad.astype(BF16)

    shape = hidden.shape
    outs = (shape, F32), (shape, BF16)
    return simple(middle_back_kernel, outs, place, hidden, grads, *parts, vec)


def leave(n_parts, place, values, rows, outs):
    blocks = [take_features(n_parts, values, s).astype(BF16) for s in range(N)]
    for t, out_ref in enumerate(outs):
        value = blocks[0]
        for s in range(1, N):
            value = jnp.where(place[1] ^ t == s, blocks[s], value)
        out_ref[rows, :] = value


def finish(n_parts, place, hidden, parts, x, grad_hidden, grad_parts, vec):
    size = hidden.shape[0]

    def finish_kernel(place, h_ref, a_ref, b_ref, c_ref, x_ref, g_ref, d_ref, e_ref, f_ref, vec_ref, *outs):
        values = h_ref[...] + summed(a_ref, b_ref, c_ref) + vec_ref[5:6, :]
        leave(n_parts, place, values, slice(0, size), outs)
        values = x_ref[...].astype(F32)
        grad = norm_backward(summed(d_ref, e_ref, f_ref), values, vec_ref[0:1, :])
        leave(n_parts, place, g_ref[...] + grad, slice(size, 2 * size), outs)

    outs = (((2 * size, hidden.shape[1] // N), BF16),) * N
    args = hidden, *parts, x, grad_hidden, *grad_parts, vec
    return simple(finish_kernel, outs, place, *args)


def stack_tokens(place, pieces):
    rows, cols = pieces[0].shape[0] // 2, pieces[0].shape[1]

    def stack_kernel(place, *refs):
        *pieces, a_ref, b_ref = refs
        for j in range(N):
            value = choose(place[3] ^ j, pieces)
            at = slice(j * rows, (j + 1) * rows)
            a_ref[at, :] = value[:rows]
            b_ref[at, :] = value[rows:].astype(F32)

    outs = ((N * rows, cols), BF16), ((N * rows, cols), F32)
    return simple(stack_kernel, outs, place, *pieces)


def pp_y(v):
    return lax.ppermute(v, "col", [(i, i ^ 2) for i in range(N)])


def pp_c(v):
    return lax.ppermute(v, "col", [(i, i ^ 1) for i in range(N)])


def pp_x(v):
    return lax.ppermute(v, "dp", [(0, 1), (1, 0)])


def pp_z(v, s):
    return lax.ppermute(v, "row", [(i, (i + s) % N) for i in range(N)])


def swap_all(axis, pieces):
    pairs = lambda t: [(i, i ^ t) for i in range(N)]
    return [pieces[0]] + [lax.ppermute(pieces[t], axis, pairs(t)) for t in range(1, N)]


def gather_weight(shard):
    if lax.axis_size("dp") != 2:
        return [lax.all_gather(shard, "row", axis=0, tiled=True)]
    size = shard.shape[0] // 2
    own = lax.dynamic_slice_in_dim(shard, lax.axis_index("dp") * size, size, 0)
    got = [pp_z(own, s) for s in range(1, N)]
    return [shard] + got + [pp_x(g) for g in got]


def reduce_weight(place, sent, kept, extra=False):
    got = pp_x(sent)
    return sum_rows(place, *combine(place, kept, got), extra=extra)


def sum_rows(place, total, *pieces, extra=False):
    got = [pp_z(piece, s + 1) for s, piece in enumerate(pieces)]
    outs = ((total.shape, BF16),)
    if extra:
        size = total.shape[0] - EXTRA
        outs = ((size, total.shape[1]), BF16), ((EXTRA, total.shape[1]), F32)

    def total_kernel(place, own_ref, a_ref, b_ref, c_ref, *outs):
        total = own_ref[...] + a_ref[...].astype(F32) + summed_low(b_ref, c_ref)
        size = outs[0].shape[0]
        outs[0][...] = total[:size].astype(BF16)
        if extra:
            outs[1][...] = total[size:]

    return simple(total_kernel, outs, place, total, *got)


def summed_low(first_ref, second_ref):
    return first_ref[...].astype(F32) + second_ref[...].astype(F32)


def flipped_sum(place, first, second):
    def flip_kernel(place, a_ref, b_ref, out_ref):
        out_ref[...] = (a_ref[...].astype(F32) + b_ref[...].astype(F32)).T

    return simple(flip_kernel, ((first.shape[::-1], F32),), place, first, second)[0]


def joined_parts(place, own, other):
    rows, cols = own.shape

    def join_kernel(place, a_ref, b_ref, out_ref):
        first = place[0] == 0
        out_ref[:rows, :] = jnp.where(first, a_ref[...], b_ref[...]).astype(F32)
        out_ref[rows:, :] = jnp.where(first, b_ref[...], a_ref[...]).astype(F32)

    return simple(join_kernel, (((2 * rows, cols), F32),), place, own, other)[0]


def both_parts(total):
    other = pp_x(total)
    x = lax.axis_index("dp")
    first, second = jnp.where(x == 0, total, other), jnp.where(x == 0, other, total)
    return jnp.concatenate([first, second], axis=0).astype(F32)


def gather_tokens(values):
    far = pp_y(values)
    return values, pp_c(values), far, pp_c(far)


def reduce_tokens(near, near_other, far, far_other):
    far = (far + pp_c(far_other).astype(F32)).astype(BF16)
    return near, pp_c(near_other), pp_y(far)


def three_terms(values):
    high = lax.reduce_precision(values, 8, 7)
    rest = values - high
    middle = lax.reduce_precision(rest, 8, 7)
    return [term.astype(BF16) for term in (high, middle, rest - middle)]


def body(
    block_input,
    w_qkv,
    b_qv,
    w_out,
    b_out,
    gain_one,
    shift_one,
    gain_two,
    shift_two,
    w_up,
    b_up,
    w_down,
    b_down,
    cotangent,
):
    r, c = lax.axis_index("row"), lax.axis_index("col")
    two = lax.axis_size("dp") == 2
    n_parts = 2 if two else 1
    x = lax.axis_index("dp") if two else 0 * r
    place = jnp.stack([x, r, c % 2, c]).astype(jnp.int32)
    width_row = block_input.shape[1]
    width_col = w_qkv.shape[2]
    hidden_col = w_up.shape[1]

    vectors = jnp.stack([gain_one, shift_one, gain_two, shift_two, b_out, b_down])
    n_vec = vectors.shape[0]
    extra = jnp.concatenate(three_terms(vectors), axis=0)
    extra = jnp.pad(extra, ((0, 32 - 3 * n_vec), (0, 0)))
    pieces = swap_all("col", split_tokens(place, block_input, cotangent))
    pieces = swap_all("row", turn_tokens(place, pieces, extra))
    inputs, grads, vec, normed_one = enter(n_parts, place, pieces, n_vec)
    gain_one, shift_one, gain_two, shift_two = vec[0], vec[1], vec[2], vec[3]

    weight_a = beside(place, w_qkv.reshape(width_row, 3 * width_col), w_out)
    weight_a = assemble(place, gather_weight(weight_a))
    weight_b = beside(place, w_up, w_down)
    weight_b = assemble(place, gather_weight(weight_b))

    ones = gather_tokens(normed_one)
    cots = gather_tokens(grads)
    bias = jnp.concatenate([b_qv[0], jnp.zeros_like(b_qv[0]), b_qv[1]])[None]

    proj_near, att_near, lse_near, *near = attend(place, *ones[:2], weight_a, bias)
    proj_far, att_far, lse_far, *far = attend(place, *ones[2:], weight_a, bias)
    hidden, normed_two = middle(place, inputs, reduce_tokens(*near, *far), vec)

    twos = gather_tokens(normed_two)
    fed_near = feed(place, *twos[:2], *cots[:2], weight_b, b_up[None])
    fed_far = feed(place, *twos[2:], *cots[2:], weight_b, b_up[None])
    act_near, pre_near, *near, sum_near, feat_near = fed_near
    act_far, pre_far, *far, sum_far, feat_far = fed_far
    grad_two = reduce_tokens(*near[2:], *far[2:])
    if two:
        (down_grad,) = sum_rows(place, *weight_rows(place, cots, act_near, act_far))
        grad_w_down = flipped_sum(place, down_grad, pp_x(down_grad))
    else:
        down_grad = weight_grad(place, (cots, act_near, act_far, hidden_col, 0))
    up_grad = weight_grad(place, (twos, pre_near, pre_far, hidden_col, 0))
    fed = reduce_tokens(*near[:2], *far[:2])

    grad_b_up = sum_near + sum_far
    products, grad_shift_two = feat_near[0] + feat_far[0], feat_near[1] + feat_far[1]
    grad_gain_two = (products - shift_two * grad_shift_two) / gain_two
    grad_b_down = feat_near[2]

    grad_hidden, branch = middle_back(place, hidden, grads, grad_two, vec)
    branches = gather_tokens(branch)
    gp_near, *near, sum_near, feat_near = attend_back(
        place, *branches[:2], *ones[:2], weight_a, proj_near, lse_near
    )
    gp_far, *far, sum_far, feat_far = attend_back(
        place, *branches[2:], *ones[2:], weight_a, proj_far, lse_far
    )
    grad_one = reduce_tokens(*near, *far)
    sums = (sum_near + sum_far).reshape(3, width_col)
    grad_b_qv = jnp.concatenate([sums[0], sums[2]])[None]
    products, grad_shift_one = feat_near[0] + feat_far[0], feat_near[1] + feat_far[1]
    grad_gain_one = (products - shift_one * grad_shift_one) / gain_one
    zeros = jnp.zeros_like(shift_one)
    by_feature = jnp.stack(
        [
            grad_gain_one,
            grad_shift_one,
            grad_gain_two,
            grad_shift_two,
            feat_near[2],
            grad_b_down,
            zeros,
            zeros,
        ]
    )
    pieces = finish(n_parts, place, hidden, fed, inputs, grad_hidden, grad_one, vec)
    pieces = swap_all("row", pieces)
    pieces = swap_all("col", turn_tokens(place, pieces))
    block_output, grad_input = stack_tokens(place, pieces)

    head = 2 * width_col
    first_terms = ((ones, gp_near, gp_far, head, 0),)
    last_terms = (ones, gp_near, gp_far, width_col, 2), (branches, att_near, att_far, width_col, 0)
    if two:
        first_grad = weight_grad(place, *first_terms, extra=(by_feature, grad_b_up, grad_b_qv))
        last_grad = weight_grad(place, *last_terms)
        first_grad, sums = reduce_weight(place, *first_grad, extra=True)
        (last_grad,) = reduce_weight(place, *last_grad)
        (up_grad,) = reduce_weight(place, *up_grad)
        own = first_grad.shape[0]
        sums = (sums[0:10:2] + sums[1:10:2]).reshape(1, -1)
        grad_b_up, grad_b_qv = sums[:, :hidden_col], sums[:, hidden_col : hidden_col + head]
        by_feature = sums[:, hidden_col + head :]
        by_feature = by_feature + pp_c(by_feature)
        by_feature = by_feature + pp_y(by_feature)
        other = pp_x(by_feature)
        first = jnp.where(x == 0, by_feature, other).reshape(-1, own)
        second = jnp.where(x == 0, other, by_feature).reshape(-1, own)
        by_feature = jnp.concatenate([first, second], axis=1)
        first_grad = both_parts(first_grad)
        last_grad = both_parts(last_grad)
        grad_w_up = joined_parts(place, up_grad, pp_x(up_grad))
    else:

        def reduced(sent, kept):
            whole = jnp.concatenate([kept, sent.astype(F32)], axis=0)
            part = lax.psum_scatter(whole, "row", scatter_dimension=0, tiled=True)
            return lax.psum(part, "dp")

        first_grad = reduced(*weight_grad(place, *first_terms))
        last_grad = reduced(*weight_grad(place, *last_terms))
        grad_w_down, grad_w_up = reduced(*down_grad).T, reduced(*up_grad)
        grad_b_up, grad_b_qv = lax.psum((grad_b_up, grad_b_qv), ("dp", "row"))
        by_feature = lax.psum(by_feature, ("dp", "row", "col"))
        by_feature = lax.dynamic_slice_in_dim(by_feature, r * width_row, width_row, 1)
    grad_w_qkv = jnp.concatenate([first_grad, last_grad[:, :width_col]], axis=1)
    grad_w_qkv = grad_w_qkv.reshape(width_row, 3, width_col)
    grad_w_out = last_grad[:, width_col:].T
    grad_b_up = grad_b_up[0]
    grad_b_qv = grad_b_qv.reshape(2, width_col)
    return (
        block_output,
        grad_input,
        grad_w_qkv,
        grad_b_qv,
        grad_w_out,
        by_feature[4],
        by_feature[0],
        by_feature[1],
        by_feature[2],
        by_feature[3],
        grad_w_up,
        grad_b_up,
        grad_w_down,
        by_feature[5],
    )


def solution(mesh):
    assert mesh.shape["row"] == N and mesh.shape["col"] == N
    tokens = P(("dp", "col"), "row")
    placed = (
        tokens,
        P("row", None, "col"),
        P(None, "col"),
        P("col", "row"),
        P("row"),
        P("row"),
        P("row"),
        P("row"),
        P("row"),
        P("row", "col"),
        P("col"),
        P("col", "row"),
        P("row"),
        tokens,
    )
    return jax.shard_map(
        body,
        mesh=mesh,
        in_specs=placed,
        out_specs=(tokens, tokens) + placed[1:13],
        check_vma=False,
    )
```

```python
import jax
import jax.numpy as jnp
from jax import lax
from jax.experimental import pallas as pl
from jax.experimental.pallas import tpu as pltpu
from jax.sharding import PartitionSpec as P


HD = 64
LEN = 512
EPS = 1e-05
MASKED = -1e30
F32 = jnp.float32
BF16 = jnp.bfloat16
N = 4
EXTRA = 16


def dot(a, b, ca=1, cb=0):
    return lax.dot_general(a, b, (((ca,), (cb,)), ((), ())), preferred_element_type=F32)


def head_mask(shape, h):
    return lax.broadcasted_iota(jnp.int32, shape, 1) // HD == h


def attn_fwd(core, proj_ref, out_ref, lse_ref):
    half, width = LEN // 2, out_ref.shape[1]
    r0 = pl.ds(pl.multiple_of(core * half, half), half)
    r1 = pl.ds(pl.multiple_of((1 - core) * half, half), half)
    q0, q1 = proj_ref[r0, :width], proj_ref[r1, :width]
    k0, k1 = proj_ref[r0, width : 2 * width], proj_ref[r1, width : 2 * width]
    v0, v1 = proj_ref[r0, 2 * width :], proj_ref[r1, 2 * width :]
    tri = lax.broadcasted_iota(jnp.int32, (half, half), 1) <= lax.broadcasted_iota(
        jnp.int32, (half, half), 0
    )
    out0 = jnp.zeros((half, width), F32)
    out1 = jnp.zeros((half, width), F32)
    lse0 = jnp.zeros((half, 128), F32)
    lse1 = jnp.zeros((half, 128), F32)
    lane = lax.broadcasted_iota(jnp.int32, (half, 128), 1)
    for h in range(width // HD):
        mask = head_mask((half, width), h)
        zero = jnp.zeros((half, width), BF16)
        qh0, qh1 = jnp.where(mask, q0, zero), jnp.where(mask, q1, zero)
        vh0, vh1 = jnp.where(mask, v0, zero), jnp.where(mask, v1, zero)
        s00 = jnp.where(tri, dot(qh0, k0, 1, 1) * 0.125, MASKED)
        top = jnp.max(s00, axis=1, keepdims=True)
        e00 = jnp.exp(s00 - top)
        total = jnp.sum(e00, axis=1, keepdims=True)
        out0 += dot((e00 / total).astype(BF16), vh0)
        lse0 = jnp.where(lane == h, top + jnp.log(total), lse0)
        s10 = dot(qh1, k0, 1, 1) * 0.125
        s11 = jnp.where(tri, dot(qh1, k1, 1, 1) * 0.125, MASKED)
        top = jnp.maximum(
            jnp.max(s10, axis=1, keepdims=True), jnp.max(s11, axis=1, keepdims=True)
        )
        e10, e11 = jnp.exp(s10 - top), jnp.exp(s11 - top)
        total = jnp.sum(e10, axis=1, keepdims=True) + jnp.sum(e11, axis=1, keepdims=True)
        out1 += dot((e10 / total).astype(BF16), vh0) + dot((e11 / total).astype(BF16), vh1)
        lse1 = jnp.where(lane == h, top + jnp.log(total), lse1)
    out_ref[r0, :] = out0.astype(BF16)
    out_ref[r1, :] = out1.astype(BF16)
    lse_ref[r0, :] = lse0
    lse_ref[r1, :] = lse1


def attn_bwd(core, proj_ref, lse_ref, grad_ref, out_ref):
    half, width = LEN // 2, grad_ref.shape[1]
    r0 = pl.ds(pl.multiple_of(core * half, half), half)
    r1 = pl.ds(pl.multiple_of((1 - core) * half, half), half)
    q0, q1 = proj_ref[r0, :width], proj_ref[r1, :width]
    k0, k1 = proj_ref[r0, width : 2 * width], proj_ref[r1, width : 2 * width]
    v0, v1 = proj_ref[r0, 2 * width :], proj_ref[r1, 2 * width :]
    g0, g1 = grad_ref[r0, :], grad_ref[r1, :]
    lse0, lse1 = lse_ref[r0, :], lse_ref[r1, :]
    tri = lax.broadcasted_iota(jnp.int32, (half, half), 1) <= lax.broadcasted_iota(
        jnp.int32, (half, half), 0
    )
    zeros = jnp.zeros((half, width), F32)
    dq0, dq1, dk0, dk1, dv0, dv1 = (zeros,) * 6
    for h in range(width // HD):
        mask = head_mask((half, width), h)
        zero = jnp.zeros((half, width), BF16)
        qh0, qh1 = jnp.where(mask, q0, zero), jnp.where(mask, q1, zero)
        kh0, kh1 = jnp.where(mask, k0, zero), jnp.where(mask, k1, zero)
        gh0, gh1 = jnp.where(mask, g0, zero), jnp.where(mask, g1, zero)
        l0, l1 = lse0[:, h : h + 1], lse1[:, h : h + 1]
        p00 = jnp.exp(jnp.where(tri, dot(qh0, k0, 1, 1) * 0.125, MASKED) - l0)
        d00 = dot(gh0, v0, 1, 1)
        inner = jnp.sum(p00 * d00, axis=1, keepdims=True)
        t00 = (p00 * (d00 - inner)).astype(BF16)
        p10 = jnp.exp(dot(qh1, k0, 1, 1) * 0.125 - l1)
        p11 = jnp.exp(jnp.where(tri, dot(qh1, k1, 1, 1) * 0.125, MASKED) - l1)
        d10, d11 = dot(gh1, v0, 1, 1), dot(gh1, v1, 1, 1)
        inner = jnp.sum(p10 * d10, axis=1, keepdims=True) + jnp.sum(
            p11 * d11, axis=1, keepdims=True
        )
        t10 = (p10 * (d10 - inner)).astype(BF16)
        t11 = (p11 * (d11 - inner)).astype(BF16)
        p00, p10, p11 = p00.astype(BF16), p10.astype(BF16), p11.astype(BF16)
        dv0 += dot(p00, gh0, 0, 0) + dot(p10, gh1, 0, 0)
        dv1 += dot(p11, gh1, 0, 0)
        dq0 += dot(t00, kh0)
        dq1 += dot(t10, kh0) + dot(t11, kh1)
        dk0 += dot(t00, qh0, 0, 0) + dot(t10, qh1, 0, 0)
        dk1 += dot(t11, qh1, 0, 0)
    out_ref[r0, :width] = (dq0 * 0.125).astype(BF16)
    out_ref[r1, :width] = (dq1 * 0.125).astype(BF16)
    out_ref[r0, width : 2 * width] = (dk0 * 0.125).astype(BF16)
    out_ref[r1, width : 2 * width] = (dk1 * 0.125).astype(BF16)
    out_ref[r0, 2 * width :] = dv0.astype(BF16)
    out_ref[r1, 2 * width :] = dv1.astype(BF16)


SMEM = pl.BlockSpec(memory_space=pltpu.SMEM)
VMEM = pl.BlockSpec(memory_space=pltpu.VMEM)
ANY = pl.BlockSpec(memory_space=pl.ANY)


def shaped(shape, dtype):
    return jax.ShapeDtypeStruct(shape, dtype)


def vmem(mib=24):
    return pltpu.CompilerParams(vmem_limit_bytes=mib << 20)


def cost(flops):
    return pl.CostEstimate(flops=flops, transcendentals=0, bytes_accessed=4 << 20)


def piece_copies(place, refs, whole_ref, sems):
    x, r = place[0], place[1]
    own, *got = refs
    size = own.shape[0] // 2
    out = []

    def copy(source, part, row):
        at = pl.multiple_of((part * N + row) * size, size)
        out.append(pltpu.make_async_copy(source, whole_ref.at[pl.ds(at, size), :], sems.at[len(out)]))

    for p in range(2):
        copy(own.at[pl.ds(p * size, size), :], p, r)
    for s in range(1, N):
        copy(got[s - 1], x, (r + N - s) % N)
        copy(got[N - 2 + s], 1 - x, (r + N - s) % N)
    return out


def assemble(place, pieces):
    if len(pieces) == 1:
        return pieces[0]
    own = pieces[0]

    def assemble_kernel(place, *refs):
        *pieces, whole_ref, sems = refs
        copies = piece_copies(place, pieces, whole_ref, sems)
        for copy in copies:
            copy.start()
        for copy in copies:
            copy.wait()

    return pl.pallas_call(
        assemble_kernel,
        out_shape=shaped((N * own.shape[0], own.shape[1]), BF16),
        in_specs=[SMEM] + [ANY] * len(pieces),
        out_specs=VMEM,
        scratch_shapes=[pltpu.SemaphoreType.DMA((8,))],
        compiler_params=vmem(),
        cost_estimate=cost(1 << 20),
        name="assemble",
    )(place, *pieces)


def attend_kernel(
    place, a_ref, b_ref, w_ref, bias_ref, proj_ref, att_ref, lse_ref, p0_ref, p1_ref
):
    rows, wide = a_ref.shape[0], proj_ref.shape[1]
    weight = w_ref[:, :wide]
    both = jnp.concatenate([a_ref[...], b_ref[...]], axis=0)
    proj_ref[...] = (dot(both, weight) + bias_ref[...]).astype(BF16)
    attn_fwd(place[2], proj_ref, att_ref, lse_ref)
    weight = w_ref[:, wide:]
    part = dot(att_ref[...], weight, 1, 1)
    p0_ref[...] = part[:rows]
    p1_ref[...] = part[rows:].astype(BF16)


def attend(place, a, b, weight, bias):
    rows, width = a.shape
    wide = bias.shape[1]
    head = wide // 3
    return pl.pallas_call(
        attend_kernel,
        out_shape=(
            shaped((2 * rows, wide), BF16),
            shaped((2 * rows, head), BF16),
            shaped((2 * rows, 128), F32),
            shaped((rows, width), F32),
            shaped((rows, width), BF16),
        ),
        in_specs=[SMEM] + [VMEM] * 4,
        out_specs=(VMEM,) * 5,
        compiler_params=vmem(),
        cost_estimate=cost(16 * rows * width * width),
        name="attend",
    )(place, a, b, weight, bias)


def attend_back_kernel(place, *refs):
    a_ref, b_ref, na_ref, nb_ref, w_ref, proj_ref, lse_ref, *refs = refs
    gp_ref, p0_ref, p1_ref, sum_ref, feat_ref, grad_ref = refs
    rows, wide = a_ref.shape[0], proj_ref.shape[1]
    weight = w_ref[:, wide:]
    both = jnp.concatenate([a_ref[...], b_ref[...]], axis=0)
    grad_ref[...] = dot(both, weight).astype(BF16)
    attn_bwd(place[2], proj_ref, lse_ref, grad_ref, gp_ref)
    weight = w_ref[:, :wide]
    part = dot(gp_ref[...], weight, 1, 1)
    p0_ref[...] = part[:rows]
    p1_ref[...] = part[rows:].astype(BF16)
    sum_ref[...] = jnp.sum(gp_ref[...].astype(F32), axis=0, keepdims=True)
    feature_sums(feat_ref, part, na_ref, nb_ref, a_ref)


def feature_sums(feat_ref, part, na_ref, nb_ref, own_ref):
    normed = jnp.concatenate([na_ref[...], nb_ref[...]], axis=0).astype(F32)
    feat_ref[0:1, :] = jnp.sum(part * normed, axis=0, keepdims=True)
    feat_ref[1:2, :] = jnp.sum(part, axis=0, keepdims=True)
    feat_ref[2:3, :] = jnp.sum(own_ref[...].astype(F32), axis=0, keepdims=True)
    feat_ref[3:, :] = jnp.zeros((feat_ref.shape[0] - 3, feat_ref.shape[1]), F32)


def attend_back(place, a, b, na, nb, weight, proj, lse):
    rows, width = a.shape
    wide = proj.shape[1]
    return pl.pallas_call(
        attend_back_kernel,
        out_shape=(
            shaped((2 * rows, wide), BF16),
            shaped((rows, width), F32),
            shaped((rows, width), BF16),
            shaped((1, wide), F32),
            shaped((8, width), F32),
        ),
        in_specs=[SMEM] + [VMEM] * 7,
        out_specs=(VMEM,) * 5,
        scratch_shapes=[pltpu.VMEM((2 * rows, wide // 3), BF16)],
        compiler_params=vmem(),
        cost_estimate=cost(24 * rows * width * width),
        name="attend_back",
    )(place, a, b, na, nb, weight, proj, lse)


def feed_kernel(place, *refs):
    a_ref, b_ref, ga_ref, gb_ref, w_ref, bias_ref, *refs = refs
    act_ref, pre_ref, m0_ref, m1_ref, p0_ref, p1_ref, sum_ref, feat_ref = refs
    rows, hidden = a_ref.shape[0], act_ref.shape[1]
    size = 256
    normed = jnp.concatenate([a_ref[...], b_ref[...]], axis=0)
    grads = jnp.concatenate([ga_ref[...], gb_ref[...]], axis=0)
    for at in range(0, hidden, size):
        cols = slice(at, at + size)
        v = dot(normed, w_ref[:, cols]) + bias_ref[:, cols]
        root = 0.7978845608028654
        square = v * v
        t = jnp.tanh(root * (v + 0.044715 * (square * v)))
        half = 0.5 * (1.0 + t)
        act_ref[:, cols] = (v * half).astype(BF16)
        slope = half + 0.5 * v * (1.0 - t * t) * (root * (1.0 + 0.134145 * square))
        pre = (dot(grads, w_ref[:, hidden + at : hidden + at + size]) * slope).astype(BF16)
        pre_ref[:, cols] = pre
        sum_ref[:, cols] = jnp.sum(pre.astype(F32), axis=0, keepdims=True)
    part = dot(act_ref[...], w_ref[:, hidden:], 1, 1)
    m0_ref[...] = part[:rows]
    m1_ref[...] = part[rows:].astype(BF16)
    part = dot(pre_ref[...], w_ref[:, :hidden], 1, 1)
    p0_ref[...] = part[:rows]
    p1_ref[...] = part[rows:].astype(BF16)
    feature_sums(feat_ref, part, a_ref, b_ref, ga_ref)


def feed(place, a, b, grad_a, grad_b, weight, bias):
    rows, width = a.shape
    hidden = bias.shape[1]
    return pl.pallas_call(
        feed_kernel,
        out_shape=(
            shaped((2 * rows, hidden), BF16),
            shaped((2 * rows, hidden), BF16),
            shaped((rows, width), F32),
            shaped((rows, width), BF16),
            shaped((rows, width), F32),
            shaped((rows, width), BF16),
            shaped((1, hidden), F32),
            shaped((8, width), F32),
        ),
        in_specs=[SMEM] + [VMEM] * 6,
        out_specs=(VMEM,) * 8,
        compiler_params=vmem(),
        cost_estimate=cost(16 * rows * width * hidden),
        name="feed",
    )(place, a, b, grad_a, grad_b, weight, bias)


def weight_kernel(n_terms, place, *refs):
    terms, (*extra, sent_ref, kept_ref) = refs[: 6 * n_terms], refs[6 * n_terms :]
    step = pl.program_id(0)
    half = terms[0].shape[1]
    size = half // N
    stride = sent_ref.shape[0] // N

    def write(out_ref):
        start = 0
        for i in range(0, len(terms), 6):
            a, b, c, d, near, far = terms[i : i + 6]
            near_left = jnp.concatenate([a[...], b[...]], axis=0)
            far_left = jnp.concatenate([c[...], d[...]], axis=0)
            value = dot(near_left, near[...], 0, 0) + dot(far_left, far[...], 0, 0)
            value = value.astype(out_ref.dtype)
            cols = slice(start, start + near.shape[1])
            start = cols.stop
            for s in range(N):
                rows = slice(s * stride, s * stride + size)
                out_ref[rows, cols] = value[s * size : (s + 1) * size]
        if extra:
            write_extra(out_ref)

    def write_extra(out_ref):
        feat_ref, up_ref, qv_ref = extra
        cols = out_ref.shape[1]
        first = (place[0] + 1 + step) % 2 == 0
        for s in range(N):
            base = s * stride + size
            out_ref[base : base + EXTRA, :] = jnp.zeros((EXTRA, cols), out_ref.dtype)
            own = slice(s * size, (s + 1) * size)
            other = slice(half + s * size, half + (s + 1) * size)
            lanes = [
                jnp.where(first, feat_ref[v : v + 1, own], feat_ref[v : v + 1, other])
                for v in range(8)
            ]
            row = jnp.concatenate([up_ref[...], qv_ref[...]] + lanes, axis=1)
            for i in range(row.shape[1] // cols):
                piece = row[:, i * cols : (i + 1) * cols]
                high = piece.astype(BF16).astype(F32)
                at = base + 2 * i
                out_ref[at : at + 1, :] = high.astype(out_ref.dtype)
                out_ref[at + 1 : at + 2, :] = (piece - high).astype(out_ref.dtype)

    @pl.when(step == 0)
    def _():
        write(sent_ref)

    @pl.when(step == 1)
    def _():
        write(kept_ref)


def weight_grad(place, *terms, extra=()):
    args, specs, cols = [], [], 0
    rows, width = terms[0][0][0].shape
    half = width // 2
    for pieces, near, far, size, at in terms:
        args += [*pieces, near, far]
        specs += [pl.BlockSpec((rows, half), lambda i, ref: (0, (ref[0] + 1 + i) % 2))] * 4
        specs += [pl.BlockSpec((2 * rows, size), lambda i, ref, at=at: (0, at))] * 2
        cols += size
    specs += [pl.BlockSpec(e.shape, lambda i, ref: (0, 0)) for e in extra]
    tall = half + N * EXTRA if extra else half
    whole = pl.BlockSpec((tall, cols), lambda i, ref: (0, 0))
    return pl.pallas_call(
        lambda *refs: weight_kernel(len(terms), *refs),
        grid_spec=pltpu.PrefetchScalarGridSpec(
            num_scalar_prefetch=1, grid=(2,), in_specs=specs, out_specs=(whole, whole)
        ),
        out_shape=(shaped((tall, cols), BF16), shaped((tall, cols), F32)),
        compiler_params=vmem(),
        cost_estimate=cost(8 * rows * width * cols),
        name="weight_grad",
    )(place, *args, *extra)


def rows_kernel(place, a, b, c, d, near, far, *refs):
    *outs, value_ref = refs
    near_left = jnp.concatenate([a[...], b[...]], axis=0)
    far_left = jnp.concatenate([c[...], d[...]], axis=0)
    value_ref[...] = dot(near_left, near[...], 0, 0) + dot(far_left, far[...], 0, 0)
    size = value_ref.shape[0] // N
    to = pl.ds(pl.multiple_of(pl.program_id(0) * size, size), size)
    for shift, out_ref in enumerate(outs):
        at = pl.ds(pl.multiple_of(((place[1] + shift) % N) * size, size), size)
        out_ref[to, :] = value_ref[at, :].astype(out_ref.dtype)


def weight_rows(place, pieces, near, far, cols):
    rows, width = pieces[0].shape
    half = width // 2
    specs = [pl.BlockSpec((rows, half), lambda i, ref: (0, i))] * 4
    specs += [pl.BlockSpec((2 * rows, cols), lambda i, ref: (0, 0))] * 2
    whole = pl.BlockSpec((width // N, cols), lambda i, ref: (0, 0))
    out = shaped((width // N, cols), BF16)
    return pl.pallas_call(
        rows_kernel,
        grid_spec=pltpu.PrefetchScalarGridSpec(
            num_scalar_prefetch=1,
            grid=(2,),
            in_specs=specs,
            out_specs=(whole,) * N,
            scratch_shapes=[pltpu.VMEM((half, cols), F32)],
        ),
        out_shape=(shaped((width // N, cols), F32),) + (out,) * (N - 1),
        compiler_params=vmem(),
        cost_estimate=cost(8 * rows * width * cols),
        name="weight_rows",
    )(place, *pieces, near, far)


def combine_kernel(place, kept_ref, got_ref, own_ref, *outs):
    size, r = own_ref.shape[0], place[1]

    def block(shift):
        at = pl.ds(pl.multiple_of(((r + shift) % N) * size, size), size)
        return kept_ref[at, :] + got_ref[at, :].astype(F32)

    own_ref[...] = block(0)
    for shift, out_ref in enumerate(outs):
        out_ref[...] = block(shift + 1).astype(BF16)


def combine(place, kept, got):
    size, cols = kept.shape[0] // N, kept.shape[1]
    return pl.pallas_call(
        combine_kernel,
        out_shape=(shaped((size, cols), F32),) + (shaped((size, cols), BF16),) * (N - 1),
        in_specs=[SMEM, VMEM, VMEM],
        out_specs=(VMEM,) * N,
        compiler_params=vmem(),
        cost_estimate=cost(1 << 20),
        name="combine",
    )(place, kept, got)


def simple(kernel, outs, *args):
    return pl.pallas_call(
        kernel,
        out_shape=tuple(shaped(shape, dtype) for shape, dtype in outs),
        in_specs=[SMEM] + [VMEM] * (len(args) - 1),
        out_specs=(VMEM,) * len(outs),
        compiler_params=vmem(),
        cost_estimate=cost(1 << 20),
    )(*args)


def beside(place, first, second):
    rows, cols = first.shape[0], first.shape[1] + second.shape[0]

    def beside_kernel(place, a_ref, b_ref, out_ref):
        out_ref[:, : a_ref.shape[1]] = a_ref[...]
        out_ref[:, a_ref.shape[1] :] = b_ref[...].T

    return simple(beside_kernel, (((rows, cols), BF16),), place, first, second)[0]


def choose(index, refs, rows=slice(None)):
    value = refs[0][rows, :]
    for i in range(1, len(refs)):
        value = jnp.where(index == i, refs[i][rows, :], value)
    return value


def put_features(n_parts, out_ref, block, s, rows=slice(None)):
    size = block.shape[1] // n_parts
    for p in range(n_parts):
        at = (p * N + s) * size
        out_ref[rows, at : at + size] = block[:, p * size : (p + 1) * size]


def take_features(n_parts, values, s):
    size = values.shape[1] // N // n_parts
    parts = [values[:, (p * N + s) * size : (p * N + s + 1) * size] for p in range(n_parts)]
    return jnp.concatenate(parts, axis=1)


def moments(values):
    centred = values - jnp.mean(values, axis=1, keepdims=True)
    scale = lax.rsqrt(jnp.mean(centred * centred, axis=1, keepdims=True) + EPS)
    return centred * scale, scale


def enter(n_parts, place, pieces, n_vec):
    rows, width = (pieces[0].shape[0] - 32) // 2, pieces[0].shape[1] * N

    def enter_kernel(place, *refs):
        *pieces, x_ref, g_ref, vec_ref, normed_ref = refs
        vec_ref[...] = jnp.zeros_like(vec_ref)
        for s in range(N):
            block = choose(place[1] ^ s, pieces)
            put_features(n_parts, x_ref, block[:rows], s)
            put_features(n_parts, g_ref, block[rows : 2 * rows], s)
            terms = block[2 * rows :].astype(F32)
            vec = terms[:n_vec] + terms[n_vec : 2 * n_vec] + terms[2 * n_vec : 3 * n_vec]
            put_features(n_parts, vec_ref, vec, s, slice(0, n_vec))
        normal, _ = moments(x_ref[...].astype(F32))
        normed_ref[...] = (normal * vec_ref[0:1, :] + vec_ref[1:2, :]).astype(BF16)

    tokens = (rows, width), BF16
    outs = tokens, tokens, ((8, width), F32), tokens
    return simple(enter_kernel, outs, place, *pieces)


def split_tokens(place, first, second):
    rows, cols = first.shape[0] // N, first.shape[1]

    def split_kernel(place, a_ref, b_ref, *outs):
        for s, out_ref in enumerate(outs):
            at = pl.ds(pl.multiple_of((place[3] ^ s) * rows, rows), rows)
            out_ref[:rows, :] = a_ref[at, :]
            out_ref[rows:, :] = b_ref[at, :]

    return simple(split_kernel, (((2 * rows, cols), BF16),) * N, place, first, second)


def turn_tokens(place, pieces, extra=None):
    rows, cols = pieces[0].shape
    more = () if extra is None else (extra,)

    def turn_kernel(place, *refs):
        for t, out_ref in enumerate(refs[N + len(more) :]):
            out_ref[:rows, :] = choose(place[3] ^ place[1] ^ t, refs[:N])
            if more:
                out_ref[rows:, :] = refs[N][...]

    outs = (((rows + sum(e.shape[0] for e in more), cols), BF16),) * N
    return simple(turn_kernel, outs, place, *pieces, *more)


def summed(first_ref, second_ref, third_ref):
    return first_ref[...] + second_ref[...].astype(F32) + third_ref[...].astype(F32)


def middle(place, x, parts, vec):
    def middle_kernel(place, x_ref, a_ref, b_ref, c_ref, vec_ref, hidden_ref, normed_ref):
        hidden = x_ref[...].astype(F32) + summed(a_ref, b_ref, c_ref) + vec_ref[4:5, :]
        hidden_ref[...] = hidden
        normal, _ = moments(hidden)
        normed_ref[...] = (normal * vec_ref[2:3, :] + vec_ref[3:4, :]).astype(BF16)

    return simple(middle_kernel, ((x.shape, F32), (x.shape, BF16)), place, x, *parts, vec)


def norm_backward(grad, values, gain):
    normal, scale = moments(values)
    scaled = grad * gain
    mean = jnp.mean(scaled, axis=1, keepdims=True)
    inner = jnp.mean(scaled * normal, axis=1, keepdims=True)
    return (scaled - mean - normal * inner) * scale


def middle_back(place, hidden, grads, parts, vec):
    def middle_back_kernel(place, h_ref, g_ref, a_ref, b_ref, c_ref, vec_ref, out_ref, low_ref):
        grad = norm_backward(summed(a_ref, b_ref, c_ref), h_ref[...], vec_ref[2:3, :])
        grad = g_ref[...].astype(F32) + grad
        out_ref[...] = grad
        low_ref[...] = grad.astype(BF16)

    shape = hidden.shape
    outs = (shape, F32), (shape, BF16)
    return simple(middle_back_kernel, outs, place, hidden, grads, *parts, vec)


def leave(n_parts, place, values, rows, outs):
    blocks = [take_features(n_parts, values, s).astype(BF16) for s in range(N)]
    for t, out_ref in enumerate(outs):
        value = blocks[0]
        for s in range(1, N):
            value = jnp.where(place[1] ^ t == s, blocks[s], value)
        out_ref[rows, :] = value


def finish(n_parts, place, hidden, parts, x, grad_hidden, grad_parts, vec):
    size = hidden.shape[0]

    def finish_kernel(place, h_ref, a_ref, b_ref, c_ref, x_ref, g_ref, d_ref, e_ref, f_ref, vec_ref, *outs):
        values = h_ref[...] + summed(a_ref, b_ref, c_ref) + vec_ref[5:6, :]
        leave(n_parts, place, values, slice(0, size), outs)
        values = x_ref[...].astype(F32)
        grad = norm_backward(summed(d_ref, e_ref, f_ref), values, vec_ref[0:1, :])
        leave(n_parts, place, g_ref[...] + grad, slice(size, 2 * size), outs)

    outs = (((2 * size, hidden.shape[1] // N), BF16),) * N
    args = hidden, *parts, x, grad_hidden, *grad_parts, vec
    return simple(finish_kernel, outs, place, *args)


def stack_tokens(place, pieces):
    rows, cols = pieces[0].shape[0] // 2, pieces[0].shape[1]

    def stack_kernel(place, *refs):
        *pieces, a_ref, b_ref = refs
        for j in range(N):
            value = choose(place[3] ^ j, pieces)
            at = slice(j * rows, (j + 1) * rows)
            a_ref[at, :] = value[:rows]
            b_ref[at, :] = value[rows:].astype(F32)

    outs = ((N * rows, cols), BF16), ((N * rows, cols), F32)
    return simple(stack_kernel, outs, place, *pieces)


def pp_y(v):
    return lax.ppermute(v, "col", [(i, i ^ 2) for i in range(N)])


def pp_c(v):
    return lax.ppermute(v, "col", [(i, i ^ 1) for i in range(N)])


def pp_x(v):
    return lax.ppermute(v, "dp", [(0, 1), (1, 0)])


def pp_z(v, s):
    return lax.ppermute(v, "row", [(i, (i + s) % N) for i in range(N)])


def swap_all(axis, pieces):
    pairs = lambda t: [(i, i ^ t) for i in range(N)]
    return [pieces[0]] + [lax.ppermute(pieces[t], axis, pairs(t)) for t in range(1, N)]


def gather_weight(shard):
    if lax.axis_size("dp") != 2:
        return [lax.all_gather(shard, "row", axis=0, tiled=True)]
    size = shard.shape[0] // 2
    own = lax.dynamic_slice_in_dim(shard, lax.axis_index("dp") * size, size, 0)
    got = [pp_z(own, s) for s in range(1, N)]
    return [shard] + got + [pp_x(g) for g in got]


def reduce_weight(place, sent, kept, extra=False):
    got = pp_x(sent)
    return sum_rows(place, *combine(place, kept, got), extra=extra)


def sum_rows(place, total, *pieces, extra=False):
    got = [pp_z(piece, s + 1) for s, piece in enumerate(pieces)]
    outs = ((total.shape, BF16),)
    if extra:
        size = total.shape[0] - EXTRA
        outs = ((size, total.shape[1]), BF16), ((EXTRA, total.shape[1]), F32)

    def total_kernel(place, own_ref, a_ref, b_ref, c_ref, *outs):
        total = own_ref[...] + a_ref[...].astype(F32) + summed_low(b_ref, c_ref)
        size = outs[0].shape[0]
        outs[0][...] = total[:size].astype(BF16)
        if extra:
            outs[1][...] = total[size:]

    return simple(total_kernel, outs, place, total, *got)


def summed_low(first_ref, second_ref):
    return first_ref[...].astype(F32) + second_ref[...].astype(F32)


def flipped(place, first, second, own, other):
    size, cols = own.shape

    def flip_kernel(place, a_ref, b_ref, c_ref, d_ref, out_ref):
        out_ref[:cols, :] = (a_ref[...].astype(F32) + b_ref[...].astype(F32)).T
        low = place[0] == 0
        out_ref[cols:, :size] = jnp.where(low, c_ref[...], d_ref[...]).astype(F32).T
        out_ref[cols:, size:] = jnp.where(low, d_ref[...], c_ref[...]).astype(F32).T

    outs = (((2 * cols, 2 * size), F32),)
    return simple(flip_kernel, outs, place, first, second, own, other)[0]


def joined_parts(place, own, other):
    rows, cols = own.shape

    def join_kernel(place, a_ref, b_ref, out_ref):
        first = place[0] == 0
        out_ref[:rows, :] = jnp.where(first, a_ref[...], b_ref[...]).astype(F32)
        out_ref[rows:, :] = jnp.where(first, b_ref[...], a_ref[...]).astype(F32)

    return simple(join_kernel, (((2 * rows, cols), F32),), place, own, other)[0]


def both_parts(total):
    other = pp_x(total)
    x = lax.axis_index("dp")
    first, second = jnp.where(x == 0, total, other), jnp.where(x == 0, other, total)
    return jnp.concatenate([first, second], axis=0).astype(F32)


def gather_tokens(values):
    far = pp_y(values)
    return values, pp_c(values), far, pp_c(far)


def reduce_tokens(near, near_other, far, far_other):
    far = (far + pp_c(far_other).astype(F32)).astype(BF16)
    return near, pp_c(near_other), pp_y(far)


def three_terms(values):
    high = lax.reduce_precision(values, 8, 7)
    rest = values - high
    middle = lax.reduce_precision(rest, 8, 7)
    return [term.astype(BF16) for term in (high, middle, rest - middle)]


def body(
    block_input,
    w_qkv,
    b_qv,
    w_out,
    b_out,
    gain_one,
    shift_one,
    gain_two,
    shift_two,
    w_up,
    b_up,
    w_down,
    b_down,
    cotangent,
):
    r, c = lax.axis_index("row"), lax.axis_index("col")
    two = lax.axis_size("dp") == 2
    n_parts = 2 if two else 1
    x = lax.axis_index("dp") if two else 0 * r
    place = jnp.stack([x, r, c % 2, c]).astype(jnp.int32)
    width_row = block_input.shape[1]
    width_col = w_qkv.shape[2]
    hidden_col = w_up.shape[1]

    vectors = jnp.stack([gain_one, shift_one, gain_two, shift_two, b_out, b_down])
    n_vec = vectors.shape[0]
    extra = jnp.concatenate(three_terms(vectors), axis=0)
    extra = jnp.pad(extra, ((0, 32 - 3 * n_vec), (0, 0)))
    pieces = swap_all("col", split_tokens(place, block_input, cotangent))
    pieces = swap_all("row", turn_tokens(place, pieces, extra))
    inputs, grads, vec, normed_one = enter(n_parts, place, pieces, n_vec)
    gain_one, shift_one, gain_two, shift_two = vec[0], vec[1], vec[2], vec[3]

    weight_a = beside(place, w_qkv.reshape(width_row, 3 * width_col), w_out)
    weight_a = assemble(place, gather_weight(weight_a))
    weight_b = beside(place, w_up, w_down)
    weight_b = assemble(place, gather_weight(weight_b))

    ones = gather_tokens(normed_one)
    cots = gather_tokens(grads)
    bias = jnp.concatenate([b_qv[0], jnp.zeros_like(b_qv[0]), b_qv[1]])[None]

    proj_near, att_near, lse_near, *near = attend(place, *ones[:2], weight_a, bias)
    proj_far, att_far, lse_far, *far = attend(place, *ones[2:], weight_a, bias)
    hidden, normed_two = middle(place, inputs, reduce_tokens(*near, *far), vec)

    twos = gather_tokens(normed_two)
    fed_near = feed(place, *twos[:2], *cots[:2], weight_b, b_up[None])
    fed_far = feed(place, *twos[2:], *cots[2:], weight_b, b_up[None])
    act_near, pre_near, *near, sum_near, feat_near = fed_near
    act_far, pre_far, *far, sum_far, feat_far = fed_far
    grad_two = reduce_tokens(*near[2:], *far[2:])
    if two:
        part = hidden_col // 2
        down_rows = weight_rows(place, cots, act_near, act_far, part)
        (down_rows,) = sum_rows(place, *down_rows)
        down_half = weight_grad(place, (cots, act_near, act_far, part, 1))
        (down_half,) = reduce_weight(place, *down_half)
        down_parts = down_rows, pp_x(down_rows), down_half, pp_x(down_half)
        grad_w_down = flipped(place, *down_parts)
    else:
        down_grad = weight_grad(place, (cots, act_near, act_far, hidden_col, 0))
    up_grad = weight_grad(place, (twos, pre_near, pre_far, hidden_col, 0))
    fed = reduce_tokens(*near[:2], *far[:2])

    grad_b_up = sum_near + sum_far
    products, grad_shift_two = feat_near[0] + feat_far[0], feat_near[1] + feat_far[1]
    grad_gain_two = (products - shift_two * grad_shift_two) / gain_two
    grad_b_down = feat_near[2]

    grad_hidden, branch = middle_back(place, hidden, grads, grad_two, vec)
    branches = gather_tokens(branch)
    gp_near, *near, sum_near, feat_near = attend_back(
        place, *branches[:2], *ones[:2], weight_a, proj_near, lse_near
    )
    gp_far, *far, sum_far, feat_far = attend_back(
        place, *branches[2:], *ones[2:], weight_a, proj_far, lse_far
    )
    grad_one = reduce_tokens(*near, *far)
    sums = (sum_near + sum_far).reshape(3, width_col)
    grad_b_qv = jnp.concatenate([sums[0], sums[2]])[None]
    products, grad_shift_one = feat_near[0] + feat_far[0], feat_near[1] + feat_far[1]
    grad_gain_one = (products - shift_one * grad_shift_one) / gain_one
    zeros = jnp.zeros_like(shift_one)
    by_feature = jnp.stack(
        [
            grad_gain_one,
            grad_shift_one,
            grad_gain_two,
            grad_shift_two,
            feat_near[2],
            grad_b_down,
            zeros,
            zeros,
        ]
    )
    pieces = finish(n_parts, place, hidden, fed, inputs, grad_hidden, grad_one, vec)
    pieces = swap_all("row", pieces)
    pieces = swap_all("col", turn_tokens(place, pieces))
    block_output, grad_input = stack_tokens(place, pieces)

    head = 2 * width_col
    first_terms = ((ones, gp_near, gp_far, head, 0),)
    last_terms = (ones, gp_near, gp_far, width_col, 2), (branches, att_near, att_far, width_col, 0)
    if two:
        first_grad = weight_grad(place, *first_terms, extra=(by_feature, grad_b_up, grad_b_qv))
        last_grad = weight_grad(place, *last_terms)
        first_grad, sums = reduce_weight(place, *first_grad, extra=True)
        (last_grad,) = reduce_weight(place, *last_grad)
        (up_grad,) = reduce_weight(place, *up_grad)
        own = first_grad.shape[0]
        sums = (sums[0:10:2] + sums[1:10:2]).reshape(1, -1)
        grad_b_up, grad_b_qv = sums[:, :hidden_col], sums[:, hidden_col : hidden_col + head]
        by_feature = sums[:, hidden_col + head :]
        by_feature = by_feature + pp_c(by_feature)
        by_feature = by_feature + pp_y(by_feature)
        other = pp_x(by_feature)
        first = jnp.where(x == 0, by_feature, other).reshape(-1, own)
        second = jnp.where(x == 0, other, by_feature).reshape(-1, own)
        by_feature = jnp.concatenate([first, second], axis=1)
        first_grad = both_parts(first_grad)
        last_grad = both_parts(last_grad)
        grad_w_up = joined_parts(place, up_grad, pp_x(up_grad))
    else:

        def reduced(sent, kept):
            whole = jnp.concatenate([kept, sent.astype(F32)], axis=0)
            part = lax.psum_scatter(whole, "row", scatter_dimension=0, tiled=True)
            return lax.psum(part, "dp")

        first_grad = reduced(*weight_grad(place, *first_terms))
        last_grad = reduced(*weight_grad(place, *last_terms))
        grad_w_down, grad_w_up = reduced(*down_grad).T, reduced(*up_grad)
        grad_b_up, grad_b_qv = lax.psum((grad_b_up, grad_b_qv), ("dp", "row"))
        by_feature = lax.psum(by_feature, ("dp", "row", "col"))
        by_feature = lax.dynamic_slice_in_dim(by_feature, r * width_row, width_row, 1)
    grad_w_qkv = jnp.concatenate([first_grad, last_grad[:, :width_col]], axis=1)
    grad_w_qkv = grad_w_qkv.reshape(width_row, 3, width_col)
    grad_w_out = last_grad[:, width_col:].T
    grad_b_up = grad_b_up[0]
    grad_b_qv = grad_b_qv.reshape(2, width_col)
    return (
        block_output,
        grad_input,
        grad_w_qkv,
        grad_b_qv,
        grad_w_out,
        by_feature[4],
        by_feature[0],
        by_feature[1],
        by_feature[2],
        by_feature[3],
        grad_w_up,
        grad_b_up,
        grad_w_down,
        by_feature[5],
    )


def solution(mesh):
    assert mesh.shape["row"] == N and mesh.shape["col"] == N
    tokens = P(("dp", "col"), "row")
    placed = (
        tokens,
        P("row", None, "col"),
        P(None, "col"),
        P("col", "row"),
        P("row"),
        P("row"),
        P("row"),
        P("row"),
        P("row"),
        P("row", "col"),
        P("col"),
        P("col", "row"),
        P("row"),
        tokens,
    )
    return jax.shard_map(
        body,
        mesh=mesh,
        in_specs=placed,
        out_specs=(tokens, tokens) + placed[1:13],
        check_vma=False,
    )
```
